128 devices in a mesh: loop: 32 (over y, x, z_lo), cross: 4 (over z_hi, core).
Axes of the slice: x: 4, y: 4, z: 4 (z_hi: 2, z_lo: 2; z = z_hi * 2 + z_lo), core: 2. Of those that a mesh axis runs over, the one named last changes fastest.
Arguments:
- populations: float32 [27, 256, 128, 128], P(None, 'loop', 'cross'), may hold values from 0 to 1, as said below
- scalars: float32 [14, 256, 128, 128], P(None, 'loop', 'cross'), may hold values from 0 to 1, as said below
- node_flags: int32 [256, 128, 128], P('loop', 'cross'), may hold values from 0 to 4, as said below
Outputs:
- new_populations: float32 [27, 256, 128, 128], P(None, 'loop', 'cross')
- new_scalars: float32 [14, 256, 128, 128], P(None, 'loop', 'cross')
The draws below stay inside these ranges and needn't reach their ends.
Inputs may be any that keep to these rules, and one draw needn't show every extreme that they name: `node_flags`: every cell in the first or last layer along either cross-section dimension is a wall. `populations`: all entries positive. `scalars`: all entries positive.
All inputs are finite; a program needn't handle non-finite values.
Results may differ from the reference program's by a relative error of at most 0.0001.
Values sent between devices are 32-bit elements; how exact they have to be, the bound alone decides.
A program may use at most 128 MiB of HBM per device.

```python
import jax
import jax.numpy as jnp
from jax import lax

NZ = 128
NX = 256
NY = 128


def flow_table():
    dirs_list = [(a, b, c) for a in (-1, 0, 1) for b in (-1, 0, 1) for c in (-1, 0, 1)]
    table = {0: 8.0 / 27.0, 1: 2.0 / 27.0, 2: 1.0 / 54.0, 3: 1.0 / 216.0}
    return (dirs_list, [table[abs(a) + abs(b) + abs(c)] for a, b, c in dirs_list])


def draw_populations(key, part):
    keys = jax.random.split(jax.random.fold_in(key, 11), 3)
    shape = (NX, NY, NZ)
    density = jax.random.uniform(keys[0], shape, jnp.float32, 0.8, 1.2)
    noise = jax.random.uniform(keys[2], (27,) + shape, jnp.float32, -0.2, 0.2)
    speed = jax.random.uniform(keys[1], (3,) + shape, jnp.float32, -0.1, 0.1)
    usq = speed[0] * speed[0] + speed[1] * speed[1] + speed[2] * speed[2]
    dirs_list, weights = flow_table()
    result = []
    for index, (a, b, c) in enumerate(dirs_list):
        proj = a * speed[0] + b * speed[1] + c * speed[2]
        feq = weights[index] * density * (1.0 + 3.0 * proj + 4.5 * proj * proj - 1.5 * usq)
        result.append(feq * (1.0 + noise[index]))
    return jnp.stack(result).astype(jnp.float32)


def draw_scalars(key, part):
    keys = jax.random.split(jax.random.fold_in(key, 23), 4)
    shape = (NX, NY, NZ)
    temp = jax.random.uniform(keys[0], shape, jnp.float32, 0.5, 1.5)
    solv = jax.random.uniform(keys[1], shape, jnp.float32, 0.2, 1.0)
    speed = jax.random.uniform(keys[2], (3,) + shape, jnp.float32, -0.1, 0.1)
    noise = jax.random.uniform(keys[3], (14,) + shape, jnp.float32, -0.2, 0.2)
    vectors = [(0, 0, 0), (1, 0, 0), (-1, 0, 0), (0, 1, 0), (0, -1, 0), (0, 0, 1), (0, 0, -1)]
    sweights = [0.25, 0.125, 0.125, 0.125, 0.125, 0.125, 0.125]
    heat = []
    solvent = []
    for index, (a, b, c) in enumerate(vectors):
        factor = 1.0 + 4.0 * (a * speed[0] + b * speed[1] + c * speed[2])
        heat.append(sweights[index] * temp * factor * (1.0 + noise[index]))
        solvent.append(sweights[index] * solv * factor * (1.0 + noise[7 + index]))
    return jnp.stack(heat + solvent).astype(jnp.float32)


def draw_node_flags(key, part):
    shape = (NX, NY, NZ)
    rolls = jax.random.randint(jax.random.fold_in(key, 37), shape, 0, 100)
    kinds = jnp.where(rolls < 70, 0, jnp.where(rolls < 80, 1, jnp.where(rolls < 87, 2, jnp.where(rolls < 94, 3, 4))))
    rows = lax.broadcasted_iota(jnp.int32, shape, 1)
    depth = lax.broadcasted_iota(jnp.int32, shape, 2)
    border = (rows == 0) | (rows == NY - 1) | (depth == 0) | (depth == NZ - 1)
    return jnp.where(border, 1, kinds).astype(jnp.int32)


def setup_inputs(seed: int = 0) -> dict:
    arg_keys = jax.random.split(jax.random.key(seed), 4)
    populations = draw_populations(jax.random.fold_in(arg_keys[3], 71), 0)
    scalars = draw_scalars(jax.random.fold_in(arg_keys[3], 71), 0)
    node_flags = draw_node_flags(jax.random.fold_in(arg_keys[3], 71), 0)
    return dict(populations=populations, scalars=scalars, node_flags=node_flags)


relax_flow = 0.8
relax_heat = 0.9
relax_solvent = 1.1
fan_speed = 0.05
heater_temp = 2.0


def flow_dirs():
    return [(a, b, c) for a in (-1, 0, 1) for b in (-1, 0, 1) for c in (-1, 0, 1)]


def flow_weights():
    table = {0: 8.0 / 27.0, 1: 2.0 / 27.0, 2: 1.0 / 54.0, 3: 1.0 / 216.0}
    return [table[abs(a) + abs(b) + abs(c)] for (a, b, c) in flow_dirs()]


def scalar_dirs():
    return [(0, 0, 0), (1, 0, 0), (-1, 0, 0), (0, 1, 0), (0, -1, 0), (0, 0, 1), (0, 0, -1)]


def scalar_opposite():
    return [0, 2, 1, 4, 3, 6, 5]


def scalar_weights():
    return [0.25, 0.125, 0.125, 0.125, 0.125, 0.125, 0.125]


def collide(pops, scal, flags):
    flow = flow_dirs()
    weights = flow_weights()
    wall = flags == 1
    fan = flags == 2
    heater = flags == 3
    exhaust = flags == 4
    density = jnp.sum(pops, axis=0)
    denom = jnp.where(wall, 1.0, density)
    table = jnp.array(flow, dtype=jnp.float32)
    mom_x = jnp.sum(pops * table[:, 0][:, None, None, None], axis=0)
    mom_y = jnp.sum(pops * table[:, 1][:, None, None, None], axis=0)
    mom_z = jnp.sum(pops * table[:, 2][:, None, None, None], axis=0)
    vel_x = jnp.where(fan, fan_speed, mom_x / denom)
    vel_y = jnp.where(fan, 0.0, mom_y / denom)
    vel_z = jnp.where(fan, 0.0, mom_z / denom)
    rho_eq = jnp.where(exhaust, 1.0, density)
    usq = vel_x * vel_x + vel_y * vel_y + vel_z * vel_z
    out_flow = []
    for index, (a, b, c) in enumerate(flow):
        proj = a * vel_x + b * vel_y + c * vel_z
        feq = weights[index] * rho_eq * (1.0 + 3.0 * proj + 4.5 * proj * proj - 1.5 * usq)
        relaxed = pops[index] - (pops[index] - feq) / relax_flow
        forced = jnp.where(fan | exhaust, feq, relaxed)
        out_flow.append(jnp.where(wall, pops[26 - index], forced))
    temp = jnp.sum(scal[0:7], axis=0)
    solv = jnp.sum(scal[7:14], axis=0)
    heat_out = []
    solv_out = []
    opposite = scalar_opposite()
    sweights = scalar_weights()
    for index, (a, b, c) in enumerate(scalar_dirs()):
        proj = a * vel_x + b * vel_y + c * vel_z
        factor = 1.0 + 4.0 * proj
        geq = sweights[index] * temp * factor
        hot = sweights[index] * heater_temp * factor
        relaxed = scal[index] - (scal[index] - geq) / relax_heat
        heat_out.append(jnp.where(wall, scal[opposite[index]], jnp.where(heater, hot, relaxed)))
        heq = sweights[index] * solv * factor
        relaxed = scal[7 + index] - (scal[7 + index] - heq) / relax_solvent
        solv_out.append(jnp.where(wall, scal[7 + opposite[index]], jnp.where(exhaust, 0.0, relaxed)))
    return jnp.stack(out_flow), jnp.stack(heat_out + solv_out)


def stream_field(field, vectors):
    result = []
    for index, (a, b, c) in enumerate(vectors):
        comp = field[index]
        size_x, size_y, size_z = comp.shape
        wide = jnp.concatenate([comp[-1:], comp, comp[:1]], axis=0)
        wide = jnp.pad(wide, ((0, 0), (1, 1), (1, 1)))
        result.append(wide[1 - a:1 - a + size_x, 1 - b:1 - b + size_y, 1 - c:1 - c + size_z])
    return jnp.stack(result)


def reference(populations, scalars, node_flags):
    pops = populations
    scal = scalars
    for step in range(2):
        post_flow, post_scal = collide(pops, scal, node_flags)
        pops = stream_field(post_flow, flow_dirs())
        scal = stream_field(post_scal, scalar_dirs() + scalar_dirs())
    return pops, scal
```

```python
import functools

import jax
import jax.numpy as jnp
from jax import lax
from jax.experimental import pallas as pl
from jax.experimental.pallas import tpu as pltpu
from jax.sharding import PartitionSpec as P

MESH = pl.DeviceIdType.MESH

FLOW = [(a, b, c) for a in (-1, 0, 1) for b in (-1, 0, 1) for c in (-1, 0, 1)]
SCAL = [(0, 0, 0), (1, 0, 0), (-1, 0, 0), (0, 1, 0), (0, -1, 0), (0, 0, 1), (0, 0, -1)]
SCAL_OPP = [0, 2, 1, 4, 3, 6, 5]
STATE = FLOW + SCAL + SCAL

ORDER = [i for a in (-1, 0, 1) for i in range(41) if STATE[i][0] == a]
SLOT = [ORDER.index(i) for i in range(41)]
LOW = (0, 11)
HIGH = (30, 41)
ROWS = [[i for i in range(41) if STATE[i][1] == b] for b in (-1, 1)]
EDGES = [(a, b) for a in (-1, 1) for b in (-1, 1)]
EDGE_FIELDS = [[i for i in range(27) if STATE[i][:2] == ab] for ab in EDGES]


def collide(load, flag, emit):
    f = [load(i) for i in range(27)]
    wall = flag == 1
    fan = flag == 2
    heater = flag == 3
    exhaust = flag == 4
    line, diff = {}, {}
    for a in range(3):
        for b in range(3):
            lo, mid, hi = f[9 * a + 3 * b], f[9 * a + 3 * b + 1], f[9 * a + 3 * b + 2]
            line[a, b] = (lo + hi) + mid
            diff[a, b] = hi - lo
    plane = [(line[a, 0] + line[a, 2]) + line[a, 1] for a in range(3)]
    rho = (plane[0] + plane[2]) + plane[1]
    mom_x = plane[2] - plane[0]
    mom_y = (line[0, 2] - line[0, 0]) + (line[2, 2] - line[2, 0]) + (line[1, 2] - line[1, 0])
    mom_z = (
        ((diff[0, 0] + diff[0, 1]) + (diff[0, 2] + diff[1, 0]))
        + ((diff[1, 1] + diff[1, 2]) + (diff[2, 0] + diff[2, 1]))
        + diff[2, 2]
    )
    inv = 1.0 / jnp.where(wall, 1.0, rho)
    ux = jnp.where(fan, 0.05, mom_x * inv)
    uy = jnp.where(fan, 0.0, mom_y * inv)
    uz = jnp.where(fan, 0.0, mom_z * inv)
    forced = fan | exhaust
    alpha = jnp.where(forced, 0.0, -0.25)
    scale = jnp.where(exhaust, 1.0, rho) * jnp.where(forced, 1.0 / 216.0, 1.25 / 216.0)
    usq = ux * ux + uy * uy + uz * uz
    v = (1.5 * ux, 1.5 * uy, 1.5 * uz)
    base1 = scale * (1.0 - 1.5 * usq)
    base = {0: 64.0 * base1, 1: 16.0 * base1, 2: 4.0 * base1, 3: base1}
    doubled = scale + scale
    q1 = tuple(doubled * t for t in v)
    q = {3: q1, 2: tuple(4.0 * t for t in q1), 1: tuple(16.0 * t for t in q1)}

    def signed(vec, direction, cache):
        if direction in cache:
            return cache[direction]
        nonzero = [n for n in range(3) if direction[n]]
        if len(nonzero) == 1:
            out = vec[nonzero[0]]
        else:
            head = list(direction)
            head[nonzero[-1]] = 0
            first = signed(vec, tuple(head), cache)
            last = vec[nonzero[-1]]
            out = first + last if direction[nonzero[-1]] > 0 else first - last
        cache[direction] = out
        return out

    vcache, qcache = {}, {1: {}, 2: {}, 3: {}}
    emit(13, jnp.where(wall, f[13], alpha * f[13] + base[0]))
    for i in range(14, 27):
        direction = FLOW[i]
        kind = sum(abs(n) for n in direction)
        odd = signed(q[kind], direction, qcache[kind])
        even = base[kind] + odd * signed(v, direction, vcache)
        opp = 26 - i
        emit(i, jnp.where(wall, f[opp], alpha * f[i] + (even + odd)))
        emit(opp, jnp.where(wall, f[i], alpha * f[opp] + (even - odd)))

    half = (0.5 * ux, 0.5 * uy, 0.5 * uz)
    factor = [0.25] + [0.125 + sign * half[n] for n in range(3) for sign in (1, -1)]
    for first, special in ((27, heater), (34, exhaust)):
        g = [load(first + j) for j in range(7)]
        total = ((g[0] + g[1]) + (g[2] + g[3])) + ((g[4] + g[5]) + g[6])
        if first == 27:
            keep = jnp.where(special, 0.0, 1.0 - 1.0 / 0.9)
            gain = jnp.where(special, 2.0, total * (1.0 / 0.9))
        else:
            keep = jnp.where(special, 0.0, 1.0 - 1.0 / 1.1)
            gain = jnp.where(special, 0.0, total * (1.0 / 1.1))
        for j in range(7):
            emit(first + j, jnp.where(wall, g[SCAL_OPP[j]], keep * g[j] + gain * factor[j]))


def exchange_kernel(
    nl, nc, nx, nk, chunks,
    pop_hbm, scal_hbm, flag_hbm, f2,
    pop, scal, flags, f1, row_out, row_in, edge_out, edge_in,
    load_sem, face_send, face_recv, row_send, row_recv, edge_send, edge_recv,
):
    me_l = lax.axis_index("loop")
    me_c = lax.axis_index("cross")
    right = lax.rem(me_l + 1, nl)
    left = lax.rem(me_l + nl - 1, nl)
    has_low = me_c > 0
    has_high = me_c < nc - 1
    has = (has_low, has_high)
    side = (me_c - 1, me_c + 1)
    around = (left, right)
    width = nk // chunks

    def loads(x):
        return (
            pltpu.make_async_copy(pop_hbm.at[:, x], pop.at[:, x], load_sem.at[0, x]),
            pltpu.make_async_copy(scal_hbm.at[:, x], scal.at[:, x], load_sem.at[1, x]),
            pltpu.make_async_copy(flag_hbm.at[x], flags.at[x], load_sem.at[2, x]),
        )

    def start_loads(x):
        for copy in loads(x):
            copy.start()

    def wait_loads(x):
        for copy in loads(x):
            copy.wait()

    start_loads(nx - 1)
    start_loads(0)

    @pl.loop(1, nx - 1)
    def _(x):
        start_loads(x)

    row_in[...] = jnp.zeros_like(row_in)
    edge_in[...] = jnp.zeros_like(edge_in)

    barrier = pltpu.get_barrier_semaphore()
    for l in around:
        pl.semaphore_signal(barrier, inc=1, device_id=(l, me_c), device_id_type=MESH)
    for s in range(2):

        @pl.when(has[s])
        def _():
            for l in (me_l,) + around:
                pl.semaphore_signal(barrier, inc=1, device_id=(l, side[s]), device_id_type=MESH)

    sides = lax.div(me_c + nc - 1, nc) + lax.div(2 * nc - 2 - me_c, nc)

    def wait_barrier():
        pl.semaphore_wait(barrier, 2 + 3 * sides)

    lane = lax.broadcasted_iota(jnp.int32, (8, 128), 1)
    first_lane = lane == 0
    last_lane = lane == 127

    def push(dst, x, k, i, value, clear):
        a, b, c = STATE[i]
        j = SLOT[i]
        if c:
            value = pltpu.roll(value, 1 if c > 0 else 127, 1)
            if clear:
                value = jnp.where(first_lane if c > 0 else last_lane, 0.0, value)
        if b == 0:
            dst[j, x + 1 + a, k + 1] = value
        elif b > 0:
            value = pltpu.roll(value, 1, 0)
            dst[j, x + 1 + a, k + 1, 1:8] = value[1:8]
            dst[j, x + 1 + a, k + 2, 0:1] = value[0:1]
        else:
            value = pltpu.roll(value, 7, 0)
            dst[j, x + 1 + a, k + 1, 0:7] = value[0:7]
            dst[j, x + 1 + a, k, 7:8] = value[7:8]

    def first_step(x, k):
        def load(i):
            return pop[i, x, k] if i < 27 else scal[i - 27, x, k]

        collide(load, flags[x, k], lambda i, v: push(f1, x, k, i, v, True))

    def second_step(x, k):
        collide(
            lambda i: f1[SLOT[i], x + 1, k + 1],
            flags[x, k],
            lambda i, v: push(f2, x, k, i, v, False),
        )

    def face(step, s, n):
        buf = (f1, f2)[step]
        lo, hi = (LOW, HIGH)[s]
        src, dst = ((0, nx), (nx + 1, 1))[s]
        rows = slice(1 + n * width, 1 + (n + 1) * width)
        return pltpu.make_async_remote_copy(
            src_ref=buf.at[lo:hi, src, rows],
            dst_ref=buf.at[lo:hi, dst, rows],
            send_sem=face_send.at[step, s, n],
            recv_sem=face_recv.at[step, s, n],
            device_id=(around[s], me_c),
            device_id_type=MESH,
        )

    def row(step, s):
        return pltpu.make_async_remote_copy(
            src_ref=row_out.at[step, s],
            dst_ref=row_in.at[step, s],
            send_sem=row_send.at[step, s],
            recv_sem=row_recv.at[step, s],
            device_id=(me_l, side[s]),
            device_id_type=MESH,
        )

    def edge(step, e):
        a, b = EDGES[e]
        return pltpu.make_async_remote_copy(
            src_ref=edge_out.at[step, e],
            dst_ref=edge_in.at[step, e],
            send_sem=edge_send.at[step, e],
            recv_sem=edge_recv.at[step, e],
            device_id=(around[(a + 1) // 2], side[(b + 1) // 2]),
            device_id_type=MESH,
        )

    def send_edges(step, s):
        buf = (f1, f2)[step]
        for e in (2 * s, 2 * s + 1):
            a, b = EDGES[e]
            for n, i in enumerate(EDGE_FIELDS[e]):
                tile, r = (nk + 1, 0) if b > 0 else (0, 7)
                x = nx + 1 if a > 0 else 0
                edge_out[step, e, n : n + 1] = buf[SLOT[i], x, tile, r : r + 1]

            @pl.when(has[(b + 1) // 2])
            def _():
                edge(step, e).start()

    def get_edges(step, s):
        buf = (f1, f2)[step]
        for e in (2 * s, 2 * s + 1):
            a, b = EDGES[e]

            @pl.when(has[1 - (b + 1) // 2])
            def _():
                edge(step, e).wait_recv()

            for n, i in enumerate(EDGE_FIELDS[e]):
                tile, r = (1, 0) if b > 0 else (nk, 7)
                x = 1 if a > 0 else nx
                buf[SLOT[i], x, tile, r : r + 1] = edge_in[step, e, n : n + 1]

    def send_rows(step):
        buf = (f1, f2)[step]
        for s in range(2):
            tile, r = ((0, 7), (nk + 1, 0))[s]
            for n, i in enumerate(ROWS[s]):
                for x in range(nx):
                    row_out[step, s, n, x : x + 1] = buf[SLOT[i], x + 1, tile, r : r + 1]

            @pl.when(has[s])
            def _():
                row(step, s).start()

    def get_rows(step):
        buf = (f1, f2)[step]
        for s in range(2):

            @pl.when(has[1 - s])
            def _():
                row(step, s).wait_recv()

            tile, r = ((nk, 7), (1, 0))[s]
            for n, i in enumerate(ROWS[s]):
                a = STATE[i][0]
                for x in range(max(a, 0), nx + min(a, 0)):
                    buf[SLOT[i], x + 1, tile, r : r + 1] = row_in[step, s, n, x : x + 1]

    for s, x in ((1, nx - 1), (0, 0)):
        wait_loads(x)

        @pl.loop(0, nk)
        def _(k):
            first_step(x, k)

        if s == 1:
            wait_barrier()
        for n in range(chunks):
            face(0, s, n).start()
        send_edges(0, s)

    @pl.loop(1, nx - 1)
    def _(x):
        wait_loads(x)

        @pl.loop(0, nk)
        def _(k):
            first_step(x, k)

    send_rows(0)

    @pl.loop(1, nx - 1)
    def _(x):
        @pl.loop(1, nk - 1)
        def _(k):
            second_step(x, k)

    get_rows(0)

    @pl.loop(1, nx - 1)
    def _(x):
        @pl.loop(0, 2)
        def _(n):
            second_step(x, n * (nk - 1))

    for n in range(chunks):
        for s, x in ((0, nx - 1), (1, 0)):
            face(0, s, n).wait_recv()
            if n == 0:
                get_edges(0, s)

            @pl.loop(n * width, (n + 1) * width)
            def _(k):
                second_step(x, k)

            if n > 0:
                face(1, 1 - s, n - 1).start()
            if n == chunks - 1:
                face(1, 1 - s, n).start()
                send_edges(1, 1 - s)

    send_rows(1)
    get_rows(1)
    for s in range(2):
        for n in range(chunks):
            face(1, s, n).wait_recv()
        get_edges(1, s)

    for step in range(2):
        for s in range(2):
            for n in range(chunks):
                face(step, s, n).wait_send()

            @pl.when(has[s])
            def _():
                row(step, s).wait_send()

        for e in range(4):

            @pl.when(has[e % 2])
            def _():
                edge(step, e).wait_send()


GROUPS = [(0, 0, 9), (11, 9, 9), (30, 18, 9)]


def store_kernel(nx, nk, f2, pop_hbm, scal_hbm, sem):
    copies = []
    for n, (slot, i, size) in enumerate(GROUPS):
        copies.append(
            pltpu.make_async_copy(
                f2.at[slot : slot + size, 1 : nx + 1, 1 : nk + 1],
                pop_hbm.at[i : i + size],
                sem.at[n],
            )
        )
    for j in range(14):
        copies.append(
            pltpu.make_async_copy(
                f2.at[SLOT[27 + j], 1 : nx + 1, 1 : nk + 1], scal_hbm.at[j], sem.at[3 + j]
            )
        )
    for copy in copies:
        copy.start()
    for copy in copies:
        copy.wait()


def per_device(nl, nc, populations, scalars, node_flags):
    nx, ny, nz = node_flags.shape
    nk = ny // 8
    chunks = 1
    f32 = jnp.float32
    padded = (41, nx + 2, nk + 2, 8, nz)
    dma = pltpu.SemaphoreType.DMA
    place = pltpu.with_memory_space_constraint
    hbm = pl.BlockSpec(memory_space=pltpu.HBM)
    vmem = pl.BlockSpec(memory_space=pltpu.VMEM)
    f2 = pl.pallas_call(
        functools.partial(exchange_kernel, nl, nc, nx, nk, chunks),
        out_shape=pltpu.VMEM(padded, f32),
        in_specs=[hbm] * 3,
        out_specs=vmem,
        scratch_shapes=[
            pltpu.VMEM((27, nx, nk, 8, nz), f32),
            pltpu.VMEM((14, nx, nk, 8, nz), f32),
            pltpu.VMEM((nx, nk, 8, nz), jnp.int32),
            pltpu.VMEM(padded, f32),
            pltpu.VMEM((2, 2, 11, nx, nz), f32),
            pltpu.VMEM((2, 2, 11, nx, nz), f32),
            pltpu.VMEM((2, 4, 8, nz), f32),
            pltpu.VMEM((2, 4, 8, nz), f32),
            dma((3, nx)),
            dma((2, 2, chunks)),
            dma((2, 2, chunks)),
            dma((2, 2)),
            dma((2, 2)),
            dma((2, 4)),
            dma((2, 4)),
        ],
        compiler_params=pltpu.CompilerParams(
            collective_id=0, has_side_effects=True, vmem_limit_bytes=40 * 2**20
        ),
    )(
        place(populations.reshape(27, nx, nk, 8, nz), pltpu.HBM),
        place(scalars.reshape(14, nx, nk, 8, nz), pltpu.HBM),
        place(node_flags.reshape(nx, nk, 8, nz), pltpu.HBM),
    )
    new_pop, new_scal = pl.pallas_call(
        functools.partial(store_kernel, nx, nk),
        out_shape=(
            jax.ShapeDtypeStruct((27, nx, nk, 8, nz), f32),
            jax.ShapeDtypeStruct((14, nx, nk, 8, nz), f32),
        ),
        in_specs=[vmem],
        out_specs=(hbm, hbm),
        scratch_shapes=[dma((17,))],
        compiler_params=pltpu.CompilerParams(vmem_limit_bytes=2**20),
    )(place(f2, pltpu.VMEM))
    return new_pop.reshape(27, nx, ny, nz), new_scal.reshape(14, nx, ny, nz)


def solution(mesh):
    wide = P(None, "loop", "cross", None)
    return jax.shard_map(
        functools.partial(per_device, mesh.shape["loop"], mesh.shape["cross"]),
        mesh=mesh,
        in_specs=(wide, wide, P("loop", "cross", None)),
        out_specs=(wide, wide),
        check_vma=False,
    )
```

```python
import functools

import jax
import jax.numpy as jnp
from jax import lax
from jax.experimental import pallas as pl
from jax.experimental.pallas import tpu as pltpu
from jax.sharding import PartitionSpec as P

MESH = pl.DeviceIdType.MESH

FLOW = [(a, b, c) for a in (-1, 0, 1) for b in (-1, 0, 1) for c in (-1, 0, 1)]
SCAL = [(0, 0, 0), (1, 0, 0), (-1, 0, 0), (0, 1, 0), (0, -1, 0), (0, 0, 1), (0, 0, -1)]
SCAL_OPP = [0, 2, 1, 4, 3, 6, 5]
STATE = FLOW + SCAL + SCAL

ORDER = [i for a in (-1, 0, 1) for i in range(41) if STATE[i][0] == a]
SLOT = [ORDER.index(i) for i in range(41)]
FACE = ((0, 11), (30, 41))
ROWS = [[i for i in range(41) if STATE[i][1] == b] for b in (-1, 1)]
EDGE_FIELDS = [
    [[i for i in range(27) if STATE[i][:2] == (a, b)] for b in (-1, 1)] for a in (-1, 1)
]


def collide(load, flag, emit):
    f = [load(i) for i in range(27)]
    wall = flag == 1
    fan = flag == 2
    heater = flag == 3
    exhaust = flag == 4
    line, diff = {}, {}
    for a in range(3):
        for b in range(3):
            lo, mid, hi = f[9 * a + 3 * b], f[9 * a + 3 * b + 1], f[9 * a + 3 * b + 2]
            line[a, b] = (lo + hi) + mid
            diff[a, b] = hi - lo
    plane = [(line[a, 0] + line[a, 2]) + line[a, 1] for a in range(3)]
    rho = (plane[0] + plane[2]) + plane[1]
    mom_x = plane[2] - plane[0]
    mom_y = (line[0, 2] - line[0, 0]) + (line[2, 2] - line[2, 0]) + (line[1, 2] - line[1, 0])
    mom_z = (
        ((diff[0, 0] + diff[0, 1]) + (diff[0, 2] + diff[1, 0]))
        + ((diff[1, 1] + diff[1, 2]) + (diff[2, 0] + diff[2, 1]))
        + diff[2, 2]
    )
    inv = 1.0 / jnp.where(wall, 1.0, rho)
    ux = jnp.where(fan, 0.05, mom_x * inv)
    uy = jnp.where(fan, 0.0, mom_y * inv)
    uz = jnp.where(fan, 0.0, mom_z * inv)
    forced = fan | exhaust
    alpha = jnp.where(forced, 0.0, -0.25)
    scale = jnp.where(exhaust, 1.0, rho) * jnp.where(forced, 1.0 / 216.0, 1.25 / 216.0)
    usq = ux * ux + uy * uy + uz * uz
    v = (1.5 * ux, 1.5 * uy, 1.5 * uz)
    base1 = scale * (1.0 - 1.5 * usq)
    base = {0: 64.0 * base1, 1: 16.0 * base1, 2: 4.0 * base1, 3: base1}
    doubled = scale + scale
    q1 = tuple(doubled * t for t in v)
    q = {3: q1, 2: tuple(4.0 * t for t in q1), 1: tuple(16.0 * t for t in q1)}

    def signed(vec, direction, cache):
        if direction in cache:
            return cache[direction]
        nonzero = [n for n in range(3) if direction[n]]
        if len(nonzero) == 1:
            out = vec[nonzero[0]]
        else:
            head = list(direction)
            head[nonzero[-1]] = 0
            first = signed(vec, tuple(head), cache)
            last = vec[nonzero[-1]]
            out = first + last if direction[nonzero[-1]] > 0 else first - last
        cache[direction] = out
        return out

    vcache, qcache = {}, {1: {}, 2: {}, 3: {}}
    emit(13, jnp.where(wall, f[13], alpha * f[13] + base[0]))
    for i in range(14, 27):
        direction = FLOW[i]
        kind = sum(abs(n) for n in direction)
        odd = signed(q[kind], direction, qcache[kind])
        even = base[kind] + odd * signed(v, direction, vcache)
        opp = 26 - i
        emit(i, jnp.where(wall, f[opp], alpha * f[i] + (even + odd)))
        emit(opp, jnp.where(wall, f[i], alpha * f[opp] + (even - odd)))

    half = (0.5 * ux, 0.5 * uy, 0.5 * uz)
    factor = [0.25] + [0.125 + sign * half[n] for n in range(3) for sign in (1, -1)]
    for first, special in ((27, heater), (34, exhaust)):
        g = [load(first + j) for j in range(7)]
        total = ((g[0] + g[1]) + (g[2] + g[3])) + ((g[4] + g[5]) + g[6])
        if first == 27:
            keep = jnp.where(special, 0.0, 1.0 - 1.0 / 0.9)
            gain = jnp.where(special, 2.0, total * (1.0 / 0.9))
        else:
            keep = jnp.where(special, 0.0, 1.0 - 1.0 / 1.1)
            gain = jnp.where(special, 0.0, total * (1.0 / 1.1))
        for j in range(7):
            emit(first + j, jnp.where(wall, g[SCAL_OPP[j]], keep * g[j] + gain * factor[j]))


def exchange_kernel(
    nl, nc, nx, nk,
    pop_hbm, scal_hbm, flag_hbm, f2,
    pop, scal, flags, f1, stage, arrived, row_out, row_in, edge_out, relay, edge_in,
    load_sem, face_send, face_recv, row_send, row_recv,
    relay_send, relay_recv, edge_send, edge_recv,
):
    me_l = lax.axis_index("loop")
    me_c = lax.axis_index("cross")
    around = (lax.rem(me_l + nl - 1, nl), lax.rem(me_l + 1, nl))
    side = (me_c - 1, me_c + 1)
    has = (me_c > 0, me_c < nc - 1)
    faces = (0, nx - 1)
    pieces = ((0, 1), (nk - 1, nk), (1, nk - 1))
    inner = 2

    def loads(x):
        return (
            pltpu.make_async_copy(pop_hbm.at[:, x], pop.at[:, x], load_sem.at[0, x]),
            pltpu.make_async_copy(scal_hbm.at[:, x], scal.at[:, x], load_sem.at[1, x]),
            pltpu.make_async_copy(flag_hbm.at[x], flags.at[x], load_sem.at[2, x]),
        )

    def start_loads(x):
        for copy in loads(x):
            copy.start()

    def wait_loads(x):
        for copy in loads(x):
            copy.wait()

    start_loads(nx - 1)
    start_loads(0)

    @pl.loop(1, nx - 1)
    def _(x):
        start_loads(x)

    row_in[...] = jnp.zeros_like(row_in)
    edge_in[...] = jnp.zeros_like(edge_in)

    barrier = pltpu.get_barrier_semaphore()
    for l in around:
        pl.semaphore_signal(barrier, inc=1, device_id=(l, me_c), device_id_type=MESH)
    for t in range(2):

        @pl.when(has[t])
        def _():
            pl.semaphore_signal(barrier, inc=1, device_id=(me_l, side[t]), device_id_type=MESH)

    sides = lax.div(me_c + nc - 1, nc) + lax.div(2 * nc - 2 - me_c, nc)

    def wait_barrier():
        pl.semaphore_wait(barrier, 2 + sides)

    lane = lax.broadcasted_iota(jnp.int32, (8, 128), 1)
    first_lane = lane == 0
    last_lane = lane == 127

    def put(dst, x, k, i, value):
        b = STATE[i][1]
        j = SLOT[i]
        if b == 0:
            dst[j, x + 1, k + 1] = value
        elif b > 0:
            value = pltpu.roll(value, 1, 0)
            dst[j, x + 1, k + 1, 1:8] = value[1:8]
            dst[j, x + 1, k + 2, 0:1] = value[0:1]
        else:
            value = pltpu.roll(value, 7, 0)
            dst[j, x + 1, k + 1, 0:7] = value[0:7]
            dst[j, x + 1, k, 7:8] = value[7:8]

    def first_step(x, k):
        def load(i):
            return pop[i, x, k] if i < 27 else scal[i - 27, x, k]

        def emit(i, value):
            a, _, c = STATE[i]
            if c:
                value = pltpu.roll(value, 1 if c > 0 else 127, 1)
                value = jnp.where(first_lane if c > 0 else last_lane, 0.0, value)
            put(f1, x + a, k, i, value)

        collide(load, flags[x, k], emit)

    def second_step(x, k, s=None):
        def emit(i, value):
            a, _, c = STATE[i]
            if c:
                value = pltpu.roll(value, 1 if c > 0 else 127, 1)
            if s is not None and a == 2 * s - 1:
                stage[s, SLOT[i] - FACE[s][0], k] = value
            else:
                put(f2, x + a, k, i, value)

        collide(lambda i: f1[SLOT[i], x + 1, k + 1], flags[x, k], emit)

    def face(step, s, p):
        lo, hi = FACE[s]
        first, last = pieces[p]
        if step == 0:
            rows = slice(1 + first, 1 + last)
            src = f1.at[lo:hi, (0, nx + 1)[s], rows]
            dst = f1.at[lo:hi, (nx, 1)[s], rows]
        else:
            src = stage.at[s, :, first:last]
            dst = arrived.at[s, :, first:last]
        return pltpu.make_async_remote_copy(
            src_ref=src,
            dst_ref=dst,
            send_sem=face_send.at[step, s, p],
            recv_sem=face_recv.at[step, s, p],
            device_id=(around[s], me_c),
            device_id_type=MESH,
        )

    def row(step, t):
        return pltpu.make_async_remote_copy(
            src_ref=row_out.at[step, t],
            dst_ref=row_in.at[step, t],
            send_sem=row_send.at[step, t],
            recv_sem=row_recv.at[step, t],
            device_id=(me_l, side[t]),
            device_id_type=MESH,
        )

    def hop(s, t):
        return pltpu.make_async_remote_copy(
            src_ref=edge_out.at[0, s, t],
            dst_ref=relay.at[s, t],
            send_sem=relay_send.at[s, t],
            recv_sem=relay_recv.at[s, t],
            device_id=(around[s], me_c),
            device_id_type=MESH,
        )

    def edge(step, s, t):
        return pltpu.make_async_remote_copy(
            src_ref=relay.at[s, t] if step == 0 else edge_out.at[1, s, t],
            dst_ref=edge_in.at[step, s, t],
            send_sem=edge_send.at[step, s, t],
            recv_sem=edge_recv.at[step, s, t],
            device_id=(me_l if step == 0 else around[s], side[t]),
            device_id_type=MESH,
        )

    def send_edge(step, s, t):
        for n, i in enumerate(EDGE_FIELDS[s][t]):
            if step == 0:
                tile, r = ((0, 7), (nk + 1, 0))[t]
                value = f1[SLOT[i], (0, nx + 1)[s], tile, r : r + 1]
            else:
                tile, r = ((0, 0), (nk - 1, 7))[t]
                value = stage[s, SLOT[i] - FACE[s][0], tile, r : r + 1]
            edge_out[step, s, t, n : n + 1] = value

        @pl.when(has[t])
        def _():
            (hop(s, t) if step == 0 else edge(1, s, t)).start()

    def pass_edge(s, t):
        @pl.when(has[t])
        def _():
            hop(s, t).wait_recv()
            edge(0, s, t).start()

    def get_edge(step, s, t):
        buf = (f1, f2)[step]

        @pl.when(has[1 - t])
        def _():
            edge(step, s, t).wait_recv()

        tile, r = ((nk, 7), (1, 0))[t]
        for n, i in enumerate(EDGE_FIELDS[s][t]):
            buf[SLOT[i], (nx, 1)[s], tile, r : r + 1] = edge_in[step, s, t, n : n + 1]

    def send_row(step, t):
        buf = (f1, f2)[step]
        tile, r = ((0, 7), (nk + 1, 0))[t]
        for n, i in enumerate(ROWS[t]):
            a = STATE[i][0]
            for x in range(max(a, 0), nx + min(a, 0)):
                row_out[step, t, n, x : x + 1] = buf[SLOT[i], x + 1, tile, r : r + 1]

        @pl.when(has[t])
        def _():
            row(step, t).start()

    def get_row(step, t):
        buf = (f1, f2)[step]

        @pl.when(has[1 - t])
        def _():
            row(step, t).wait_recv()

        tile, r = ((nk, 7), (1, 0))[t]
        for n, i in enumerate(ROWS[t]):
            a = STATE[i][0]
            for x in range(max(a, 0), nx + min(a, 0)):
                buf[SLOT[i], x + 1, tile, r : r + 1] = row_in[step, t, n, x : x + 1]

    for s in (1, 0):
        wait_loads(faces[s])

        @pl.loop(0, nk)
        def _(k):
            first_step(faces[s], k)

        if s == 1:
            wait_barrier()
        for t in range(2):
            send_edge(0, s, t)
        face(0, s, inner).start()

    @pl.loop(1, nx - 1)
    def _(x):
        wait_loads(x)

        @pl.loop(0, 2)
        def _(n):
            first_step(x, n * (nk - 1))

    for t in range(2):
        send_row(0, t)
    @pl.loop(1, nx - 1)
    def _(x):
        @pl.loop(1, nk - 1)
        def _(k):
            first_step(x, k)

    for s in range(2):
        for t in range(2):
            pass_edge(s, t)
    for p in range(2):
        for s in (1, 0):
            face(0, s, p).start()

    @pl.loop(1, nx - 1)
    def _(x):
        @pl.loop(1, nk - 1)
        def _(k):
            second_step(x, k)

    for s in (1, 0):
        face(0, 1 - s, inner).wait_recv()

        @pl.loop(1, nk - 1)
        def _(k):
            second_step(faces[s], k, s)

        face(1, s, inner).start()

    for p in range(2):
        k = pieces[p][0]
        get_row(0, 1 - p)

        @pl.loop(1, nx - 1)
        def _(x):
            second_step(x, k)

        for s in (1, 0):
            face(0, 1 - s, p).wait_recv()
            get_edge(0, 1 - s, 1 - p)
            second_step(faces[s], k, s)
            send_edge(1, s, p)
        send_row(1, p)
        for s in (1, 0):
            face(1, s, p).start()

    for p in (inner, 0, 1):
        for s in range(2):
            face(1, s, p).wait_recv()

            @pl.loop(*pieces[p])
            def _(k):
                for n in range(11):
                    put(f2, (nx - 1, 0)[s], k, ORDER[FACE[s][0] + n], arrived[s, n, k])

    for t in range(2):
        get_row(1, t)
        for s in range(2):
            get_edge(1, s, t)

    for step in range(2):
        for s in range(2):
            for p in range(3):
                face(step, s, p).wait_send()
        for t in range(2):

            @pl.when(has[t])
            def _():
                row(step, t).wait_send()
                for s in range(2):
                    edge(step, s, t).wait_send()
                    if step == 0:
                        hop(s, t).wait_send()


GROUPS = [(0, 0, 9), (11, 9, 9), (30, 18, 9)]


def store_kernel(nx, nk, f2, pop_hbm, scal_hbm, sem):
    copies = []
    for n, (slot, i, size) in enumerate(GROUPS):
        copies.append(
            pltpu.make_async_copy(
                f2.at[slot : slot + size, 1 : nx + 1, 1 : nk + 1],
                pop_hbm.at[i : i + size],
                sem.at[n],
            )
        )
    for j in range(14):
        copies.append(
            pltpu.make_async_copy(
                f2.at[SLOT[27 + j], 1 : nx + 1, 1 : nk + 1], scal_hbm.at[j], sem.at[3 + j]
            )
        )
    for copy in copies:
        copy.start()
    for copy in copies:
        copy.wait()


def per_device(nl, nc, populations, scalars, node_flags):
    nx, ny, nz = node_flags.shape
    nk = ny // 8
    f32 = jnp.float32
    padded = (41, nx + 2, nk + 2, 8, nz)
    dma = pltpu.SemaphoreType.DMA
    place = pltpu.with_memory_space_constraint
    hbm = pl.BlockSpec(memory_space=pltpu.HBM)
    vmem = pl.BlockSpec(memory_space=pltpu.VMEM)
    f2 = pl.pallas_call(
        functools.partial(exchange_kernel, nl, nc, nx, nk),
        out_shape=pltpu.VMEM(padded, f32),
        in_specs=[hbm] * 3,
        out_specs=vmem,
        scratch_shapes=[
            pltpu.VMEM((27, nx, nk, 8, nz), f32),
            pltpu.VMEM((14, nx, nk, 8, nz), f32),
            pltpu.VMEM((nx, nk, 8, nz), jnp.int32),
            pltpu.VMEM(padded, f32),
            pltpu.VMEM((2, 11, nk, 8, nz), f32),
            pltpu.VMEM((2, 11, nk, 8, nz), f32),
            pltpu.VMEM((2, 2, 11, nx, nz), f32),
            pltpu.VMEM((2, 2, 11, nx, nz), f32),
            pltpu.VMEM((2, 2, 2, 8, nz), f32),
            pltpu.VMEM((2, 2, 8, nz), f32),
            pltpu.VMEM((2, 2, 2, 8, nz), f32),
            dma((3, nx)),
            dma((2, 2, 3)),
            dma((2, 2, 3)),
            dma((2, 2)),
            dma((2, 2)),
            dma((2, 2)),
            dma((2, 2)),
            dma((2, 2, 2)),
            dma((2, 2, 2)),
        ],
        compiler_params=pltpu.CompilerParams(
            collective_id=0, has_side_effects=True, vmem_limit_bytes=40 * 2**20
        ),
    )(
        place(populations.reshape(27, nx, nk, 8, nz), pltpu.HBM),
        place(scalars.reshape(14, nx, nk, 8, nz), pltpu.HBM),
        place(node_flags.reshape(nx, nk, 8, nz), pltpu.HBM),
    )
    new_pop, new_scal = pl.pallas_call(
        functools.partial(store_kernel, nx, nk),
        out_shape=(
            jax.ShapeDtypeStruct((27, nx, nk, 8, nz), f32),
            jax.ShapeDtypeStruct((14, nx, nk, 8, nz), f32),
        ),
        in_specs=[vmem],
        out_specs=(hbm, hbm),
        scratch_shapes=[dma((17,))],
        compiler_params=pltpu.CompilerParams(vmem_limit_bytes=2**20),
    )(place(f2, pltpu.VMEM))
    return new_pop.reshape(27, nx, ny, nz), new_scal.reshape(14, nx, ny, nz)


def solution(mesh):
    wide = P(None, "loop", "cross", None)
    return jax.shard_map(
        functools.partial(per_device, mesh.shape["loop"], mesh.shape["cross"]),
        mesh=mesh,
        in_specs=(wide, wide, P("loop", "cross", None)),
        out_specs=(wide, wide),
        check_vma=False,
    )
```

```python
import functools

import jax
import jax.numpy as jnp
from jax import lax
from jax.experimental import pallas as pl
from jax.experimental.pallas import tpu as pltpu
from jax.sharding import PartitionSpec as P

MESH = pl.DeviceIdType.MESH

FLOW = [(a, b, c) for a in (-1, 0, 1) for b in (-1, 0, 1) for c in (-1, 0, 1)]
SCAL = [(0, 0, 0), (1, 0, 0), (-1, 0, 0), (0, 1, 0), (0, -1, 0), (0, 0, 1), (0, 0, -1)]
SCAL_OPP = [0, 2, 1, 4, 3, 6, 5]
STATE = FLOW + SCAL + SCAL

ORDER = [i for a in (-1, 0, 1) for i in range(41) if STATE[i][0] == a]
SLOT = [ORDER.index(i) for i in range(41)]
FACE = ((0, 11), (30, 41))
ROWS = [[i for i in range(41) if STATE[i][1] == b] for b in (-1, 1)]
EDGE_FIELDS = [
    [[i for i in range(27) if STATE[i][:2] == (a, b)] for b in (-1, 1)] for a in (-1, 1)
]


def collide(load, flag, emit):
    f = [load(i) for i in range(27)]
    wall = flag == 1
    fan = flag == 2
    heater = flag == 3
    exhaust = flag == 4
    line, diff = {}, {}
    for a in range(3):
        for b in range(3):
            lo, mid, hi = f[9 * a + 3 * b], f[9 * a + 3 * b + 1], f[9 * a + 3 * b + 2]
            line[a, b] = (lo + hi) + mid
            diff[a, b] = hi - lo
    plane = [(line[a, 0] + line[a, 2]) + line[a, 1] for a in range(3)]
    rho = (plane[0] + plane[2]) + plane[1]
    mom_x = plane[2] - plane[0]
    mom_y = (line[0, 2] - line[0, 0]) + (line[2, 2] - line[2, 0]) + (line[1, 2] - line[1, 0])
    mom_z = (
        ((diff[0, 0] + diff[0, 1]) + (diff[0, 2] + diff[1, 0]))
        + ((diff[1, 1] + diff[1, 2]) + (diff[2, 0] + diff[2, 1]))
        + diff[2, 2]
    )
    inv = 1.0 / jnp.where(wall, 1.0, rho)
    ux = jnp.where(fan, 0.05, mom_x * inv)
    uy = jnp.where(fan, 0.0, mom_y * inv)
    uz = jnp.where(fan, 0.0, mom_z * inv)
    forced = fan | exhaust
    alpha = jnp.where(forced, 0.0, -0.25)
    scale = jnp.where(exhaust, 1.0, rho) * jnp.where(forced, 1.0 / 216.0, 1.25 / 216.0)
    usq = ux * ux + uy * uy + uz * uz
    v = (1.5 * ux, 1.5 * uy, 1.5 * uz)
    base1 = scale * (1.0 - 1.5 * usq)
    base = {0: 64.0 * base1, 1: 16.0 * base1, 2: 4.0 * base1, 3: base1}
    doubled = scale + scale
    q1 = tuple(doubled * t for t in v)
    q = {3: q1, 2: tuple(4.0 * t for t in q1), 1: tuple(16.0 * t for t in q1)}

    def signed(vec, direction, cache):
        if direction in cache:
            return cache[direction]
        nonzero = [n for n in range(3) if direction[n]]
        if len(nonzero) == 1:
            out = vec[nonzero[0]]
        else:
            head = list(direction)
            head[nonzero[-1]] = 0
            first = signed(vec, tuple(head), cache)
            last = vec[nonzero[-1]]
            out = first + last if direction[nonzero[-1]] > 0 else first - last
        cache[direction] = out
        return out

    vcache, qcache = {}, {1: {}, 2: {}, 3: {}}
    emit(13, jnp.where(wall, f[13], alpha * f[13] + base[0]))
    for i in range(14, 27):
        direction = FLOW[i]
        kind = sum(abs(n) for n in direction)
        odd = signed(q[kind], direction, qcache[kind])
        even = base[kind] + odd * signed(v, direction, vcache)
        opp = 26 - i
        emit(i, jnp.where(wall, f[opp], alpha * f[i] + (even + odd)))
        emit(opp, jnp.where(wall, f[i], alpha * f[opp] + (even - odd)))

    half = (0.5 * ux, 0.5 * uy, 0.5 * uz)
    factor = [0.25] + [0.125 + sign * half[n] for n in range(3) for sign in (1, -1)]
    for first, special in ((27, heater), (34, exhaust)):
        g = [load(first + j) for j in range(7)]
        total = ((g[0] + g[1]) + (g[2] + g[3])) + ((g[4] + g[5]) + g[6])
        if first == 27:
            keep = jnp.where(special, 0.0, 1.0 - 1.0 / 0.9)
            gain = jnp.where(special, 2.0, total * (1.0 / 0.9))
        else:
            keep = jnp.where(special, 0.0, 1.0 - 1.0 / 1.1)
            gain = jnp.where(special, 0.0, total * (1.0 / 1.1))
        for j in range(7):
            emit(first + j, jnp.where(wall, g[SCAL_OPP[j]], keep * g[j] + gain * factor[j]))


def exchange_kernel(
    nl, nc, nx, nk,
    pop_hbm, scal_hbm, flag_hbm, f2,
    pop, scal, flags, f1, stage, arrived, row_out, row_in,
    hop_out, relay, relay_in, edge_out, edge_in,
    load_sem, face_send, face_recv, row_send, row_recv,
    hop_send, hop_recv, relay_send, relay_recv, edge_send, edge_recv,
):
    me_l = lax.axis_index("loop")
    me_c = lax.axis_index("cross")
    around = (lax.rem(me_l + nl - 1, nl), lax.rem(me_l + 1, nl))
    side = (me_c - 1, me_c + 1)
    has = (me_c > 0, me_c < nc - 1)
    faces = (0, nx - 1)
    pieces = ((0, nk // 2), (nk // 2, nk))
    ends = (0, nk - 1)
    behind = me_l == nl - 1
    ahead = me_l == 0
    level = me_l > 0
    late = jnp.logical_and(me_c == nc // 2, level)
    early = jnp.logical_and(me_c != nc // 2, level)

    def loads(x):
        return (
            pltpu.make_async_copy(pop_hbm.at[:, x], pop.at[:, x], load_sem.at[0, x]),
            pltpu.make_async_copy(scal_hbm.at[:, x], scal.at[:, x], load_sem.at[1, x]),
            pltpu.make_async_copy(flag_hbm.at[x], flags.at[x], load_sem.at[2, x]),
        )

    def start_loads(x):
        for copy in loads(x):
            copy.start()

    def wait_loads(x):
        for copy in loads(x):
            copy.wait()

    start_loads(nx - 1)
    start_loads(0)

    @pl.loop(1, nx - 1)
    def _(x):
        start_loads(x)

    row_in[...] = jnp.zeros_like(row_in)
    relay_in[...] = jnp.zeros_like(relay_in)
    edge_in[...] = jnp.zeros_like(edge_in)

    barrier = pltpu.get_barrier_semaphore()
    for l in around:
        pl.semaphore_signal(barrier, inc=1, device_id=(l, me_c), device_id_type=MESH)
    for t in range(2):

        @pl.when(has[t])
        def _():
            pl.semaphore_signal(barrier, inc=1, device_id=(me_l, side[t]), device_id_type=MESH)

    sides = lax.div(me_c + nc - 1, nc) + lax.div(2 * nc - 2 - me_c, nc)

    def wait_barrier():
        pl.semaphore_wait(barrier, 2 + sides)

    lane = lax.broadcasted_iota(jnp.int32, (8, 128), 1)
    first_lane = lane == 0
    last_lane = lane == 127

    def put(dst, x, k, i, value):
        b = STATE[i][1]
        j = SLOT[i]
        if b == 0:
            dst[j, x + 1, k + 1] = value
        elif b > 0:
            value = pltpu.roll(value, 1, 0)
            dst[j, x + 1, k + 1, 1:8] = value[1:8]
            dst[j, x + 1, k + 2, 0:1] = value[0:1]
        else:
            value = pltpu.roll(value, 7, 0)
            dst[j, x + 1, k + 1, 0:7] = value[0:7]
            dst[j, x + 1, k, 7:8] = value[7:8]

    def first_step(x, k):
        def load(i):
            return pop[i, x, k] if i < 27 else scal[i - 27, x, k]

        def emit(i, value):
            a, _, c = STATE[i]
            if c:
                value = pltpu.roll(value, 1 if c > 0 else 127, 1)
                value = jnp.where(first_lane if c > 0 else last_lane, 0.0, value)
            put(f1, x + a, k, i, value)

        collide(load, flags[x, k], emit)

    def second_step(x, k, s=None):
        def emit(i, value):
            a, _, c = STATE[i]
            if c:
                value = pltpu.roll(value, 1 if c > 0 else 127, 1)
            if s is not None and a == 2 * s - 1:
                stage[s, SLOT[i] - FACE[s][0], k] = value
            else:
                put(f2, x + a, k, i, value)

        collide(lambda i: f1[SLOT[i], x + 1, k + 1], flags[x, k], emit)

    def face(step, s, p):
        lo, hi = FACE[s]
        first, last = pieces[p]
        if step == 0:
            rows = slice(1 + first, 1 + last)
            src = f1.at[lo:hi, (0, nx + 1)[s], rows]
            dst = f1.at[lo:hi, (nx, 1)[s], rows]
        else:
            src = stage.at[s, :, first:last]
            dst = arrived.at[s, :, first:last]
        return pltpu.make_async_remote_copy(
            src_ref=src,
            dst_ref=dst,
            send_sem=face_send.at[step, s, p],
            recv_sem=face_recv.at[step, s, p],
            device_id=(around[s], me_c),
            device_id_type=MESH,
        )

    def row(step, t):
        return pltpu.make_async_remote_copy(
            src_ref=row_out.at[step, t],
            dst_ref=row_in.at[step, t],
            send_sem=row_send.at[step, t],
            recv_sem=row_recv.at[step, t],
            device_id=(me_l, side[t]),
            device_id_type=MESH,
        )

    def hop(s):
        return pltpu.make_async_remote_copy(
            src_ref=hop_out.at[s],
            dst_ref=relay.at[s],
            send_sem=hop_send.at[s],
            recv_sem=hop_recv.at[s],
            device_id=(around[s], me_c),
            device_id_type=MESH,
        )

    def forward(t):
        return pltpu.make_async_remote_copy(
            src_ref=relay,
            dst_ref=relay_in.at[t],
            send_sem=relay_send.at[t],
            recv_sem=relay_recv.at[t],
            device_id=(me_l, side[t]),
            device_id_type=MESH,
        )

    def edge(s, t):
        return pltpu.make_async_remote_copy(
            src_ref=edge_out.at[s, t],
            dst_ref=edge_in.at[s, t],
            send_sem=edge_send.at[s, t],
            recv_sem=edge_recv.at[s, t],
            device_id=(around[s], side[t]),
            device_id_type=MESH,
        )

    def pack_hop(s):
        for t in range(2):
            tile, r = ((0, 7), (nk + 1, 0))[t]
            for n, i in enumerate(EDGE_FIELDS[s][t]):
                m = 3 * t + n
                hop_out[s, m : m + 1] = f1[SLOT[i], (0, nx + 1)[s], tile, r : r + 1]

    def pass_edges():
        for s in range(2):
            hop(s).wait_recv()
        for t in range(2):

            @pl.when(has[t])
            def _():
                forward(t).start()

    def send_edge(s, t):
        tile, r = ((0, 0), (nk - 1, 7))[t]
        for n, i in enumerate(EDGE_FIELDS[s][t]):
            m = SLOT[i] - FACE[s][0]
            edge_out[s, t, n : n + 1] = stage[s, m, tile, r : r + 1]

        @pl.when(has[t])
        def _():
            edge(s, t).start()

    def get_edge(step, s, t):
        buf = (f1, f2)[step]
        if step == 1:

            @pl.when(has[1 - t])
            def _():
                edge(s, t).wait_recv()

        tile, r = ((nk, 7), (1, 0))[t]
        for n, i in enumerate(EDGE_FIELDS[s][t]):
            m = 3 * t + n
            value = relay_in[t, s, m : m + 1] if step == 0 else edge_in[s, t, n : n + 1]
            buf[SLOT[i], (nx, 1)[s], tile, r : r + 1] = value

    def pack_row(step, t):
        buf = (f1, f2)[step]
        tile, r = ((0, 7), (nk + 1, 0))[t]
        for n, i in enumerate(ROWS[t]):
            a = STATE[i][0]
            for x in range(max(a, 0), nx + min(a, 0)):
                row_out[step, t, n, x : x + 1] = buf[SLOT[i], x + 1, tile, r : r + 1]

    def send_row(step, t):
        @pl.when(has[t])
        def _():
            row(step, t).start()

    def get_row(step, t):
        buf = (f1, f2)[step]

        @pl.when(has[1 - t])
        def _():
            row(step, t).wait_recv()
            if step == 0:
                forward(t).wait_recv()

        tile, r = ((nk, 7), (1, 0))[t]
        for n, i in enumerate(ROWS[t]):
            a = STATE[i][0]
            for x in range(max(a, 0), nx + min(a, 0)):
                buf[SLOT[i], x + 1, tile, r : r + 1] = row_in[step, t, n, x : x + 1]

    def both(f, *args):
        for t in range(2):
            f(*args, t)

    def send_first(s):
        hop(s).start()
        face(0, s, 0).start()

    for s in (1, 0):
        wait_loads(faces[s])

        @pl.loop(0, nk, unroll=True)
        def _(k):
            first_step(faces[s], k)

        pack_hop(s)

        @pl.when(early)
        def _():
            if s == 1:
                wait_barrier()
            send_first(s)

    for t in range(2):

        @pl.loop(1, nx - 1)
        def _(x):
            if t == 0:
                wait_loads(x)
            first_step(x, ends[t])

        pack_row(0, t)
        pl.when(early)(lambda: send_row(0, t))

        @pl.when(late)
        def _():
            if t == 0:
                wait_barrier()
            send_row(0, t)
            if t == 0:
                for s in (1, 0):
                    send_first(s)

    @pl.loop(1, nx - 1)
    def _(x):
        @pl.loop(1, nk - 1)
        def _(k):
            first_step(x, k)

    @pl.when(ahead)
    def _():
        wait_barrier()
        for s in range(2):
            send_first(s)
        both(send_row, 0)
        for s in range(2):
            face(0, s, 1).start()

    pass_edges()

    @pl.when(level)
    def _():
        for s in (1, 0):
            face(0, s, 1).start()

    def outer(s, p):
        face(0, 1 - s, p).wait_recv()
        get_edge(0, 1 - s, 1 - p)

        @pl.loop(*pieces[p], unroll=True)
        def _(k):
            second_step(faces[s], k, s)

        send_edge(s, p)

    def between(p):
        @pl.loop(1, nx - 1)
        def _(x):
            second_step(x, ends[p])

        pack_row(1, p)
        send_row(1, p)

    for p in range(2):
        get_row(0, 1 - p)
        outer(1, p)
        face(1, 1, p).start()
        if p == 1:
            pl.when(behind)(lambda: face(1, 0, 0).start())
        outer(0, p)
        between(p)
        if p == 0:
            pl.when(jnp.logical_not(behind))(lambda: face(1, 0, 0).start())
        else:
            face(1, 0, 1).start()

    @pl.loop(1, nx - 1)
    def _(x):
        @pl.loop(1, nk - 1)
        def _(k):
            second_step(x, k)

    for p in range(2):
        for s in range(2):
            face(1, s, p).wait_recv()

            @pl.loop(*pieces[p])
            def _(k):
                for n in range(11):
                    put(f2, (nx - 1, 0)[s], k, ORDER[FACE[s][0] + n], arrived[s, n, k])

    for t in range(2):
        get_row(1, t)
        for s in range(2):
            get_edge(1, s, t)

    for s in range(2):
        hop(s).wait_send()
        for step in range(2):
            for p in range(2):
                face(step, s, p).wait_send()
    for t in range(2):

        @pl.when(has[t])
        def _():
            forward(t).wait_send()
            for s in range(2):
                row(s, t).wait_send()
                edge(s, t).wait_send()


GROUPS = [(0, 0, 9), (11, 9, 9), (30, 18, 9)]


def store_kernel(nx, nk, f2, pop_hbm, scal_hbm, sem):
    copies = []
    for n, (slot, i, size) in enumerate(GROUPS):
        copies.append(
            pltpu.make_async_copy(
                f2.at[slot : slot + size, 1 : nx + 1, 1 : nk + 1],
                pop_hbm.at[i : i + size],
                sem.at[n],
            )
        )
    for j in range(14):
        copies.append(
            pltpu.make_async_copy(
                f2.at[SLOT[27 + j], 1 : nx + 1, 1 : nk + 1], scal_hbm.at[j], sem.at[3 + j]
            )
        )
    for copy in copies:
        copy.start()
    for copy in copies:
        copy.wait()


def per_device(nl, nc, populations, scalars, node_flags):
    nx, ny, nz = node_flags.shape
    nk = ny // 8
    f32 = jnp.float32
    padded = (41, nx + 2, nk + 2, 8, nz)
    dma = pltpu.SemaphoreType.DMA
    place = pltpu.with_memory_space_constraint
    hbm = pl.BlockSpec(memory_space=pltpu.HBM)
    vmem = pl.BlockSpec(memory_space=pltpu.VMEM)
    f2 = pl.pallas_call(
        functools.partial(exchange_kernel, nl, nc, nx, nk),
        out_shape=pltpu.VMEM(padded, f32),
        in_specs=[hbm] * 3,
        out_specs=vmem,
        scratch_shapes=[
            pltpu.VMEM((27, nx, nk, 8, nz), f32),
            pltpu.VMEM((14, nx, nk, 8, nz), f32),
            pltpu.VMEM((nx, nk, 8, nz), jnp.int32),
            pltpu.VMEM(padded, f32),
            pltpu.VMEM((2, 11, nk, 8, nz), f32),
            pltpu.VMEM((2, 11, nk, 8, nz), f32),
            pltpu.VMEM((2, 2, 11, nx, nz), f32),
            pltpu.VMEM((2, 2, 11, nx, nz), f32),
            pltpu.VMEM((2, 8, nz), f32),
            pltpu.VMEM((2, 8, nz), f32),
            pltpu.VMEM((2, 2, 8, nz), f32),
            pltpu.VMEM((2, 2, 8, nz), f32),
            pltpu.VMEM((2, 2, 8, nz), f32),
            dma((3, nx)),
            dma((2, 2, 2)),
            dma((2, 2, 2)),
            dma((2, 2)),
            dma((2, 2)),
            dma((2,)),
            dma((2,)),
            dma((2,)),
            dma((2,)),
            dma((2, 2)),
            dma((2, 2)),
        ],
        compiler_params=pltpu.CompilerParams(
            collective_id=0, has_side_effects=True, vmem_limit_bytes=40 * 2**20
        ),
    )(
        place(populations.reshape(27, nx, nk, 8, nz), pltpu.HBM),
        place(scalars.reshape(14, nx, nk, 8, nz), pltpu.HBM),
        place(node_flags.reshape(nx, nk, 8, nz), pltpu.HBM),
    )
    new_pop, new_scal = pl.pallas_call(
        functools.partial(store_kernel, nx, nk),
        out_shape=(
            jax.ShapeDtypeStruct((27, nx, nk, 8, nz), f32),
            jax.ShapeDtypeStruct((14, nx, nk, 8, nz), f32),
        ),
        in_specs=[vmem],
        out_specs=(hbm, hbm),
        scratch_shapes=[dma((17,))],
        compiler_params=pltpu.CompilerParams(vmem_limit_bytes=2**20),
    )(place(f2, pltpu.VMEM))
    return new_pop.reshape(27, nx, ny, nz), new_scal.reshape(14, nx, ny, nz)


def solution(mesh):
    wide = P(None, "loop", "cross", None)
    return jax.shard_map(
        functools.partial(per_device, mesh.shape["loop"], mesh.shape["cross"]),
        mesh=mesh,
        in_specs=(wide, wide, P("loop", "cross", None)),
        out_specs=(wide, wide),
        check_vma=False,
    )
```

```python
import functools

import jax
import jax.numpy as jnp
from jax import lax
from jax.experimental import pallas as pl
from jax.experimental.pallas import tpu as pltpu
from jax.sharding import PartitionSpec as P

MESH = pl.DeviceIdType.MESH

FLOW = [(a, b, c) for a in (-1, 0, 1) for b in (-1, 0, 1) for c in (-1, 0, 1)]
SCAL = [(0, 0, 0), (1, 0, 0), (-1, 0, 0), (0, 1, 0), (0, -1, 0), (0, 0, 1), (0, 0, -1)]
SCAL_OPP = [0, 2, 1, 4, 3, 6, 5]
STATE = FLOW + SCAL + SCAL

ORDER = [i for a in (-1, 0, 1) for i in range(41) if STATE[i][0] == a]
SLOT = [ORDER.index(i) for i in range(41)]
FACE = ((0, 11), (30, 41))
ROWS = [[i for i in range(41) if STATE[i][1] == b] for b in (-1, 1)]
EDGE_FIELDS = [
    [[i for i in range(27) if STATE[i][:2] == (a, b)] for b in (-1, 1)] for a in (-1, 1)
]


def collide(load, flag, emit):
    f = [load(i) for i in range(27)]
    wall = flag == 1
    fan = flag == 2
    heater = flag == 3
    exhaust = flag == 4
    line, diff = {}, {}
    for a in range(3):
        for b in range(3):
            lo, mid, hi = f[9 * a + 3 * b], f[9 * a + 3 * b + 1], f[9 * a + 3 * b + 2]
            line[a, b] = (lo + hi) + mid
            diff[a, b] = hi - lo
    plane = [(line[a, 0] + line[a, 2]) + line[a, 1] for a in range(3)]
    rho = (plane[0] + plane[2]) + plane[1]
    mom_x = plane[2] - plane[0]
    mom_y = (line[0, 2] - line[0, 0]) + (line[2, 2] - line[2, 0]) + (line[1, 2] - line[1, 0])
    mom_z = (
        ((diff[0, 0] + diff[0, 1]) + (diff[0, 2] + diff[1, 0]))
        + ((diff[1, 1] + diff[1, 2]) + (diff[2, 0] + diff[2, 1]))
        + diff[2, 2]
    )
    inv = 1.0 / jnp.where(wall, 1.0, rho)
    ux = jnp.where(fan, 0.05, mom_x * inv)
    uy = jnp.where(fan, 0.0, mom_y * inv)
    uz = jnp.where(fan, 0.0, mom_z * inv)
    forced = fan | exhaust
    alpha = jnp.where(forced, 0.0, -0.25)
    scale = jnp.where(exhaust, 1.0, rho) * jnp.where(forced, 1.0 / 216.0, 1.25 / 216.0)
    usq = ux * ux + uy * uy + uz * uz
    v = (1.5 * ux, 1.5 * uy, 1.5 * uz)
    base1 = scale * (1.0 - 1.5 * usq)
    base = {0: 64.0 * base1, 1: 16.0 * base1, 2: 4.0 * base1, 3: base1}
    doubled = scale + scale
    q1 = tuple(doubled * t for t in v)
    q = {3: q1, 2: tuple(4.0 * t for t in q1), 1: tuple(16.0 * t for t in q1)}

    def signed(vec, direction, cache):
        if direction in cache:
            return cache[direction]
        nonzero = [n for n in range(3) if direction[n]]
        if len(nonzero) == 1:
            out = vec[nonzero[0]]
        else:
            head = list(direction)
            head[nonzero[-1]] = 0
            first = signed(vec, tuple(head), cache)
            last = vec[nonzero[-1]]
            out = first + last if direction[nonzero[-1]] > 0 else first - last
        cache[direction] = out
        return out

    vcache, qcache = {}, {1: {}, 2: {}, 3: {}}
    emit(13, jnp.where(wall, f[13], alpha * f[13] + base[0]))
    for i in range(14, 27):
        direction = FLOW[i]
        kind = sum(abs(n) for n in direction)
        odd = signed(q[kind], direction, qcache[kind])
        even = base[kind] + odd * signed(v, direction, vcache)
        opp = 26 - i
        emit(i, jnp.where(wall, f[opp], alpha * f[i] + (even + odd)))
        emit(opp, jnp.where(wall, f[i], alpha * f[opp] + (even - odd)))

    half = (0.5 * ux, 0.5 * uy, 0.5 * uz)
    factor = [0.25] + [0.125 + sign * half[n] for n in range(3) for sign in (1, -1)]
    for first, special in ((27, heater), (34, exhaust)):
        g = [load(first + j) for j in range(7)]
        total = ((g[0] + g[1]) + (g[2] + g[3])) + ((g[4] + g[5]) + g[6])
        if first == 27:
            keep = jnp.where(special, 0.0, 1.0 - 1.0 / 0.9)
            gain = jnp.where(special, 2.0, total * (1.0 / 0.9))
        else:
            keep = jnp.where(special, 0.0, 1.0 - 1.0 / 1.1)
            gain = jnp.where(special, 0.0, total * (1.0 / 1.1))
        for j in range(7):
            emit(first + j, jnp.where(wall, g[SCAL_OPP[j]], keep * g[j] + gain * factor[j]))


def exchange_kernel(
    nl, nc, nx, nk,
    pop_hbm, scal_hbm, flag_hbm, f2,
    pop, scal, flags, f1, stage, arrived, row_out, row_in,
    hop_out, relay, relay_in, edge_out, edge_in,
    load_sem, face_send, face_recv, row_send, row_recv,
    hop_send, hop_recv, relay_send, relay_recv, edge_send, edge_recv,
):
    me_l = lax.axis_index("loop")
    me_c = lax.axis_index("cross")
    around = (lax.rem(me_l + nl - 1, nl), lax.rem(me_l + 1, nl))
    side = (me_c - 1, me_c + 1)
    has = (me_c > 0, me_c < nc - 1)
    faces = (0, nx - 1)
    pieces = ((0, nk // 2), (nk // 2, nk))
    ends = (0, nk - 1)
    behind = me_l == nl - 1
    ahead = me_l == 0
    level = me_l > 0
    late = jnp.logical_and(me_c == nc // 2, level)
    early = jnp.logical_and(me_c != nc // 2, level)

    def loads(x):
        return (
            pltpu.make_async_copy(pop_hbm.at[:, x], pop.at[:, x], load_sem.at[0, x]),
            pltpu.make_async_copy(scal_hbm.at[:, x], scal.at[:, x], load_sem.at[1, x]),
            pltpu.make_async_copy(flag_hbm.at[x], flags.at[x], load_sem.at[2, x]),
        )

    def start_loads(x):
        for copy in loads(x):
            copy.start()

    def wait_loads(x):
        for copy in loads(x):
            copy.wait()

    start_loads(nx - 1)
    start_loads(0)

    row_in[...] = jnp.zeros_like(row_in)
    relay_in[...] = jnp.zeros_like(relay_in)
    edge_in[...] = jnp.zeros_like(edge_in)

    barrier = pltpu.get_barrier_semaphore()
    for l in around:
        pl.semaphore_signal(barrier, inc=1, device_id=(l, me_c), device_id_type=MESH)
    for t in range(2):

        @pl.when(has[t])
        def _():
            pl.semaphore_signal(barrier, inc=1, device_id=(me_l, side[t]), device_id_type=MESH)


    @pl.loop(1, nx - 1)
    def _(x):
        start_loads(x)

    sides = lax.div(me_c + nc - 1, nc) + lax.div(2 * nc - 2 - me_c, nc)

    def wait_barrier():
        pl.semaphore_wait(barrier, 2 + sides)

    lane = lax.broadcasted_iota(jnp.int32, (8, 128), 1)
    first_lane = lane == 0
    last_lane = lane == 127

    def put(dst, x, k, i, value):
        b = STATE[i][1]
        j = SLOT[i]
        if b == 0:
            dst[j, x + 1, k + 1] = value
        elif b > 0:
            value = pltpu.roll(value, 1, 0)
            dst[j, x + 1, k + 1, 1:8] = value[1:8]
            dst[j, x + 1, k + 2, 0:1] = value[0:1]
        else:
            value = pltpu.roll(value, 7, 0)
            dst[j, x + 1, k + 1, 0:7] = value[0:7]
            dst[j, x + 1, k, 7:8] = value[7:8]

    def first_step(x, k):
        def load(i):
            return pop[i, x, k] if i < 27 else scal[i - 27, x, k]

        def emit(i, value):
            a, _, c = STATE[i]
            if c:
                value = pltpu.roll(value, 1 if c > 0 else 127, 1)
                value = jnp.where(first_lane if c > 0 else last_lane, 0.0, value)
            put(f1, x + a, k, i, value)

        collide(load, flags[x, k], emit)

    def second_step(x, k, s=None):
        def emit(i, value):
            a, _, c = STATE[i]
            if c:
                value = pltpu.roll(value, 1 if c > 0 else 127, 1)
            if s is not None and a == 2 * s - 1:
                stage[s, SLOT[i] - FACE[s][0], k] = value
            else:
                put(f2, x + a, k, i, value)

        collide(lambda i: f1[SLOT[i], x + 1, k + 1], flags[x, k], emit)

    def face(step, s, p):
        lo, hi = FACE[s]
        first, last = pieces[p]
        if step == 0:
            rows = slice(1 + first, 1 + last)
            src = f1.at[lo:hi, (0, nx + 1)[s], rows]
            dst = f1.at[lo:hi, (nx, 1)[s], rows]
        else:
            src = stage.at[s, :, first:last]
            dst = arrived.at[s, :, first:last]
        return pltpu.make_async_remote_copy(
            src_ref=src,
            dst_ref=dst,
            send_sem=face_send.at[step, s, p],
            recv_sem=face_recv.at[step, s, p],
            device_id=(around[s], me_c),
            device_id_type=MESH,
        )

    def row(step, t):
        return pltpu.make_async_remote_copy(
            src_ref=row_out.at[step, t],
            dst_ref=row_in.at[step, t],
            send_sem=row_send.at[step, t],
            recv_sem=row_recv.at[step, t],
            device_id=(me_l, side[t]),
            device_id_type=MESH,
        )

    def hop(s):
        return pltpu.make_async_remote_copy(
            src_ref=hop_out.at[s],
            dst_ref=relay.at[s],
            send_sem=hop_send.at[s],
            recv_sem=hop_recv.at[s],
            device_id=(around[s], me_c),
            device_id_type=MESH,
        )

    def forward(t):
        return pltpu.make_async_remote_copy(
            src_ref=relay,
            dst_ref=relay_in.at[t],
            send_sem=relay_send.at[t],
            recv_sem=relay_recv.at[t],
            device_id=(me_l, side[t]),
            device_id_type=MESH,
        )

    def edge(s, t):
        return pltpu.make_async_remote_copy(
            src_ref=edge_out.at[s, t],
            dst_ref=edge_in.at[s, t],
            send_sem=edge_send.at[s, t],
            recv_sem=edge_recv.at[s, t],
            device_id=(around[s], side[t]),
            device_id_type=MESH,
        )

    def pack_hop(s):
        for t in range(2):
            tile, r = ((0, 7), (nk + 1, 0))[t]
            for n, i in enumerate(EDGE_FIELDS[s][t]):
                m = 3 * t + n
                hop_out[s, m : m + 1] = f1[SLOT[i], (0, nx + 1)[s], tile, r : r + 1]

    def pass_edges():
        for s in range(2):
            hop(s).wait_recv()
        for t in range(2):

            @pl.when(has[t])
            def _():
                forward(t).start()

    def send_edge(s, t):
        tile, r = ((0, 0), (nk - 1, 7))[t]
        for n, i in enumerate(EDGE_FIELDS[s][t]):
            m = SLOT[i] - FACE[s][0]
            edge_out[s, t, n : n + 1] = stage[s, m, tile, r : r + 1]

        @pl.when(has[t])
        def _():
            edge(s, t).start()

    def get_edge(step, s, t):
        buf = (f1, f2)[step]
        if step == 1:

            @pl.when(has[1 - t])
            def _():
                edge(s, t).wait_recv()

        tile, r = ((nk, 7), (1, 0))[t]
        for n, i in enumerate(EDGE_FIELDS[s][t]):
            m = 3 * t + n
            value = relay_in[t, s, m : m + 1] if step == 0 else edge_in[s, t, n : n + 1]
            buf[SLOT[i], (nx, 1)[s], tile, r : r + 1] = value

    def pack_row(step, t):
        buf = (f1, f2)[step]
        tile, r = ((0, 7), (nk + 1, 0))[t]
        for n, i in enumerate(ROWS[t]):
            a = STATE[i][0]
            for x in range(max(a, 0), nx + min(a, 0)):
                row_out[step, t, n, x : x + 1] = buf[SLOT[i], x + 1, tile, r : r + 1]

    def send_row(step, t):
        @pl.when(has[t])
        def _():
            row(step, t).start()

    def get_row(step, t):
        buf = (f1, f2)[step]

        @pl.when(has[1 - t])
        def _():
            row(step, t).wait_recv()
            if step == 0:
                forward(t).wait_recv()

        tile, r = ((nk, 7), (1, 0))[t]
        for n, i in enumerate(ROWS[t]):
            a = STATE[i][0]
            for x in range(max(a, 0), nx + min(a, 0)):
                buf[SLOT[i], x + 1, tile, r : r + 1] = row_in[step, t, n, x : x + 1]

    def both(f, *args):
        for t in range(2):
            f(*args, t)

    def send_first(s):
        hop(s).start()
        face(0, s, 0).start()

    for s in (1, 0):
        wait_loads(faces[s])

        @pl.loop(0, nk, unroll=True)
        def _(k):
            first_step(faces[s], k)

        pack_hop(s)

        @pl.when(early)
        def _():
            if s == 1:
                wait_barrier()
            send_first(s)

    for t in range(2):

        @pl.loop(1, nx - 1)
        def _(x):
            if t == 0:
                wait_loads(x)
            first_step(x, ends[t])

        pack_row(0, t)
        pl.when(early)(lambda: send_row(0, t))

        @pl.when(late)
        def _():
            if t == 0:
                wait_barrier()
            send_row(0, t)
            if t == 0:
                for s in (1, 0):
                    send_first(s)

    @pl.loop(1, nx - 1)
    def _(x):
        @pl.loop(1, nk - 1)
        def _(k):
            first_step(x, k)

    @pl.when(ahead)
    def _():
        wait_barrier()
        for s in range(2):
            send_first(s)
        both(send_row, 0)
        for s in range(2):
            face(0, s, 1).start()

    pass_edges()

    @pl.when(level)
    def _():
        for s in (1, 0):
            face(0, s, 1).start()

    def outer(s, p):
        face(0, 1 - s, p).wait_recv()
        get_edge(0, 1 - s, 1 - p)

        @pl.loop(*pieces[p], unroll=True)
        def _(k):
            second_step(faces[s], k, s)

        send_edge(s, p)

    def between(p):
        @pl.loop(1, nx - 1)
        def _(x):
            second_step(x, ends[p])

        pack_row(1, p)
        send_row(1, p)

    for p in range(2):
        get_row(0, 1 - p)
        outer(1, p)
        face(1, 1, p).start()
        if p == 1:
            pl.when(behind)(lambda: face(1, 0, 0).start())
        outer(0, p)
        between(p)
        if p == 0:
            pl.when(jnp.logical_not(behind))(lambda: face(1, 0, 0).start())
        else:
            face(1, 0, 1).start()

    @pl.loop(1, nx - 1)
    def _(x):
        @pl.loop(1, nk - 1)
        def _(k):
            second_step(x, k)

    for p in range(2):
        for s in range(2):
            face(1, s, p).wait_recv()

            @pl.loop(*pieces[p])
            def _(k):
                for n in range(11):
                    put(f2, (nx - 1, 0)[s], k, ORDER[FACE[s][0] + n], arrived[s, n, k])

    for t in range(2):
        get_row(1, t)
        for s in range(2):
            get_edge(1, s, t)

    for s in range(2):
        hop(s).wait_send()
        for step in range(2):
            for p in range(2):
                face(step, s, p).wait_send()
    for t in range(2):

        @pl.when(has[t])
        def _():
            forward(t).wait_send()
            for s in range(2):
                row(s, t).wait_send()
                edge(s, t).wait_send()


GROUPS = [(0, 0, 9), (11, 9, 9), (30, 18, 9)]
SCAL_GROUPS = [(SLOT[27 + j], j, size) for j, size in ((0, 1), (1, 1), (2, 1), (3, 4), (7, 1), (8, 1), (9, 1), (10, 4))]


def store_kernel(nx, nk, f2, pop_hbm, scal_hbm, sem):
    copies = []
    for n, (slot, i, size) in enumerate(GROUPS):
        copies.append(
            pltpu.make_async_copy(
                f2.at[slot : slot + size, 1 : nx + 1, 1 : nk + 1],
                pop_hbm.at[i : i + size],
                sem.at[n],
            )
        )
    for n, (slot, j, size) in enumerate(SCAL_GROUPS):
        copies.append(
            pltpu.make_async_copy(
                f2.at[slot : slot + size, 1 : nx + 1, 1 : nk + 1],
                scal_hbm.at[j : j + size],
                sem.at[3 + n],
            )
        )
    for copy in copies:
        copy.start()
    for copy in copies:
        copy.wait()


def per_device(nl, nc, populations, scalars, node_flags):
    nx, ny, nz = node_flags.shape
    nk = ny // 8
    f32 = jnp.float32
    padded = (41, nx + 2, nk + 2, 8, nz)
    dma = pltpu.SemaphoreType.DMA
    place = pltpu.with_memory_space_constraint
    hbm = pl.BlockSpec(memory_space=pltpu.HBM)
    vmem = pl.BlockSpec(memory_space=pltpu.VMEM)
    f2 = pl.pallas_call(
        functools.partial(exchange_kernel, nl, nc, nx, nk),
        out_shape=pltpu.VMEM(padded, f32),
        in_specs=[hbm] * 3,
        out_specs=vmem,
        scratch_shapes=[
            pltpu.VMEM((27, nx, nk, 8, nz), f32),
            pltpu.VMEM((14, nx, nk, 8, nz), f32),
            pltpu.VMEM((nx, nk, 8, nz), jnp.int32),
            pltpu.VMEM(padded, f32),
            pltpu.VMEM((2, 11, nk, 8, nz), f32),
            pltpu.VMEM((2, 11, nk, 8, nz), f32),
            pltpu.VMEM((2, 2, 11, nx, nz), f32),
            pltpu.VMEM((2, 2, 11, nx, nz), f32),
            pltpu.VMEM((2, 8, nz), f32),
            pltpu.VMEM((2, 8, nz), f32),
            pltpu.VMEM((2, 2, 8, nz), f32),
            pltpu.VMEM((2, 2, 8, nz), f32),
            pltpu.VMEM((2, 2, 8, nz), f32),
            dma((3, nx)),
            dma((2, 2, 2)),
            dma((2, 2, 2)),
            dma((2, 2)),
            dma((2, 2)),
            dma((2,)),
            dma((2,)),
            dma((2,)),
            dma((2,)),
            dma((2, 2)),
            dma((2, 2)),
        ],
        compiler_params=pltpu.CompilerParams(
            collective_id=0, has_side_effects=True, vmem_limit_bytes=40 * 2**20
        ),
    )(
        place(populations.reshape(27, nx, nk, 8, nz), pltpu.HBM),
        place(scalars.reshape(14, nx, nk, 8, nz), pltpu.HBM),
        place(node_flags.reshape(nx, nk, 8, nz), pltpu.HBM),
    )
    new_pop, new_scal = pl.pallas_call(
        functools.partial(store_kernel, nx, nk),
        out_shape=(
            jax.ShapeDtypeStruct((27, nx, nk, 8, nz), f32),
            jax.ShapeDtypeStruct((14, nx, nk, 8, nz), f32),
        ),
        in_specs=[vmem],
        out_specs=(hbm, hbm),
        scratch_shapes=[dma((11,))],
        compiler_params=pltpu.CompilerParams(vmem_limit_bytes=2**20),
    )(place(f2, pltpu.VMEM))
    return new_pop.reshape(27, nx, ny, nz), new_scal.reshape(14, nx, ny, nz)


def solution(mesh):
    wide = P(None, "loop", "cross", None)
    return jax.shard_map(
        functools.partial(per_device, mesh.shape["loop"], mesh.shape["cross"]),
        mesh=mesh,
        in_specs=(wide, wide, P("loop", "cross", None)),
        out_specs=(wide, wide),
        check_vma=False,
    )
```

```python
import functools

import jax
import jax.numpy as jnp
from jax import lax
from jax.experimental import pallas as pl
from jax.experimental.pallas import tpu as pltpu
from jax.sharding import PartitionSpec as P

MESH = pl.DeviceIdType.MESH

FLOW = [(a, b, c) for a in (-1, 0, 1) for b in (-1, 0, 1) for c in (-1, 0, 1)]
SCAL = [(0, 0, 0), (1, 0, 0), (-1, 0, 0), (0, 1, 0), (0, -1, 0), (0, 0, 1), (0, 0, -1)]
SCAL_OPP = [0, 2, 1, 4, 3, 6, 5]
STATE = FLOW + SCAL + SCAL

ORDER = [i for a in (-1, 0, 1) for i in range(41) if STATE[i][0] == a]
SLOT = [ORDER.index(i) for i in range(41)]
FACE = ((0, 11), (30, 41))
ROWS = [[i for i in range(41) if STATE[i][1] == b] for b in (-1, 1)]
EDGE_FIELDS = [
    [[i for i in range(27) if STATE[i][:2] == (a, b)] for b in (-1, 1)] for a in (-1, 1)
]


def collide(load, flag, emit):
    f = [load(i) for i in range(27)]
    wall = flag == 1
    fan = flag == 2
    heater = flag == 3
    exhaust = flag == 4
    line, diff = {}, {}
    for a in range(3):
        for b in range(3):
            lo, mid, hi = f[9 * a + 3 * b], f[9 * a + 3 * b + 1], f[9 * a + 3 * b + 2]
            line[a, b] = (lo + hi) + mid
            diff[a, b] = hi - lo
    plane = [(line[a, 0] + line[a, 2]) + line[a, 1] for a in range(3)]
    rho = (plane[0] + plane[2]) + plane[1]
    mom_x = plane[2] - plane[0]
    mom_y = (line[0, 2] - line[0, 0]) + (line[2, 2] - line[2, 0]) + (line[1, 2] - line[1, 0])
    mom_z = (
        ((diff[0, 0] + diff[0, 1]) + (diff[0, 2] + diff[1, 0]))
        + ((diff[1, 1] + diff[1, 2]) + (diff[2, 0] + diff[2, 1]))
        + diff[2, 2]
    )
    inv = 1.0 / jnp.where(wall, 1.0, rho)
    ux = jnp.where(fan, 0.05, mom_x * inv)
    uy = jnp.where(fan, 0.0, mom_y * inv)
    uz = jnp.where(fan, 0.0, mom_z * inv)
    forced = fan | exhaust
    alpha = jnp.where(forced, 0.0, -0.25)
    scale = jnp.where(exhaust, 1.0, rho) * jnp.where(forced, 1.0 / 216.0, 1.25 / 216.0)
    usq = ux * ux + uy * uy + uz * uz
    v = (1.5 * ux, 1.5 * uy, 1.5 * uz)
    base1 = scale * (1.0 - 1.5 * usq)
    base = {0: 64.0 * base1, 1: 16.0 * base1, 2: 4.0 * base1, 3: base1}
    doubled = scale + scale
    q1 = tuple(doubled * t for t in v)
    q = {3: q1, 2: tuple(4.0 * t for t in q1), 1: tuple(16.0 * t for t in q1)}

    def signed(vec, direction, cache):
        if direction in cache:
            return cache[direction]
        nonzero = [n for n in range(3) if direction[n]]
        if len(nonzero) == 1:
            out = vec[nonzero[0]]
        else:
            head = list(direction)
            head[nonzero[-1]] = 0
            first = signed(vec, tuple(head), cache)
            last = vec[nonzero[-1]]
            out = first + last if direction[nonzero[-1]] > 0 else first - last
        cache[direction] = out
        return out

    vcache, qcache = {}, {1: {}, 2: {}, 3: {}}
    emit(13, jnp.where(wall, f[13], alpha * f[13] + base[0]))
    for i in range(14, 27):
        direction = FLOW[i]
        kind = sum(abs(n) for n in direction)
        odd = signed(q[kind], direction, qcache[kind])
        even = base[kind] + odd * signed(v, direction, vcache)
        opp = 26 - i
        emit(i, jnp.where(wall, f[opp], alpha * f[i] + (even + odd)))
        emit(opp, jnp.where(wall, f[i], alpha * f[opp] + (even - odd)))

    half = (0.5 * ux, 0.5 * uy, 0.5 * uz)
    factor = [0.25] + [0.125 + sign * half[n] for n in range(3) for sign in (1, -1)]
    for first, special in ((27, heater), (34, exhaust)):
        g = [load(first + j) for j in range(7)]
        total = ((g[0] + g[1]) + (g[2] + g[3])) + ((g[4] + g[5]) + g[6])
        if first == 27:
            keep = jnp.where(special, 0.0, 1.0 - 1.0 / 0.9)
            gain = jnp.where(special, 2.0, total * (1.0 / 0.9))
        else:
            keep = jnp.where(special, 0.0, 1.0 - 1.0 / 1.1)
            gain = jnp.where(special, 0.0, total * (1.0 / 1.1))
        for j in range(7):
            emit(first + j, jnp.where(wall, g[SCAL_OPP[j]], keep * g[j] + gain * factor[j]))


def exchange_kernel(
    nl, nc, nx, nk,
    pop_hbm, scal_hbm, flag_hbm, f2,
    pop, scal, flags, f1, stage, arrived, row_out, row_in,
    hop_out, relay, relay_in, edge_out, edge_in,
    load_sem, face_send, face_recv, row_send, row_recv,
    hop_send, hop_recv, relay_send, relay_recv, edge_send, edge_recv,
):
    me_l = lax.axis_index("loop")
    me_c = lax.axis_index("cross")
    around = (lax.rem(me_l + nl - 1, nl), lax.rem(me_l + 1, nl))
    side = (me_c - 1, me_c + 1)
    has = (me_c > 0, me_c < nc - 1)
    faces = (0, nx - 1)
    pieces = ((0, nk // 2), (nk // 2, nk))
    ends = (0, nk - 1)
    behind = me_l == nl - 1
    ahead = me_l == 0
    level = me_l > 0
    late = jnp.logical_and(me_c == nc // 2, level)
    early = jnp.logical_and(me_c != nc // 2, level)

    def loads(x):
        return (
            pltpu.make_async_copy(pop_hbm.at[:, x], pop.at[:, x], load_sem.at[0, x]),
            pltpu.make_async_copy(scal_hbm.at[:, x], scal.at[:, x], load_sem.at[1, x]),
            pltpu.make_async_copy(flag_hbm.at[x], flags.at[x], load_sem.at[2, x]),
        )

    def start_loads(x):
        for copy in loads(x):
            copy.start()

    def wait_loads(x):
        for copy in loads(x):
            copy.wait()

    start_loads(nx - 1)
    start_loads(0)

    row_in[...] = jnp.zeros_like(row_in)
    relay_in[...] = jnp.zeros_like(relay_in)
    edge_in[...] = jnp.zeros_like(edge_in)

    barrier = pltpu.get_barrier_semaphore()
    for l in around:
        pl.semaphore_signal(barrier, inc=1, device_id=(l, me_c), device_id_type=MESH)
    for t in range(2):

        @pl.when(has[t])
        def _():
            pl.semaphore_signal(barrier, inc=1, device_id=(me_l, side[t]), device_id_type=MESH)


    @pl.loop(1, nx - 1)
    def _(x):
        start_loads(x)

    sides = lax.div(me_c + nc - 1, nc) + lax.div(2 * nc - 2 - me_c, nc)

    def wait_barrier():
        pl.semaphore_wait(barrier, 2 + sides)

    lane = lax.broadcasted_iota(jnp.int32, (8, 128), 1)
    first_lane = lane == 0
    last_lane = lane == 127

    def put(dst, x, k, i, value):
        b = STATE[i][1]
        j = SLOT[i]
        if b == 0:
            dst[j, x + 1, k + 1] = value
        elif b > 0:
            value = pltpu.roll(value, 1, 0)
            dst[j, x + 1, k + 1, 1:8] = value[1:8]
            dst[j, x + 1, k + 2, 0:1] = value[0:1]
        else:
            value = pltpu.roll(value, 7, 0)
            dst[j, x + 1, k + 1, 0:7] = value[0:7]
            dst[j, x + 1, k, 7:8] = value[7:8]

    def first_step(x, k):
        def load(i):
            return pop[i, x, k] if i < 27 else scal[i - 27, x, k]

        def emit(i, value):
            a, _, c = STATE[i]
            if c:
                value = pltpu.roll(value, 1 if c > 0 else 127, 1)
                value = jnp.where(first_lane if c > 0 else last_lane, 0.0, value)
            put(f1, x + a, k, i, value)

        collide(load, flags[x, k], emit)

    def second_step(x, k, s=None):
        def emit(i, value):
            a, _, c = STATE[i]
            if c:
                value = pltpu.roll(value, 1 if c > 0 else 127, 1)
            if s is not None and a == 2 * s - 1:
                stage[s, SLOT[i] - FACE[s][0], k] = value
            else:
                put(f2, x + a, k, i, value)

        collide(lambda i: f1[SLOT[i], x + 1, k + 1], flags[x, k], emit)

    def face(step, s, p):
        lo, hi = FACE[s]
        first, last = pieces[p]
        if step == 0:
            rows = slice(1 + first, 1 + last)
            src = f1.at[lo:hi, (0, nx + 1)[s], rows]
            dst = f1.at[lo:hi, (nx, 1)[s], rows]
        else:
            src = stage.at[s, :, first:last]
            dst = arrived.at[s, :, first:last]
        return pltpu.make_async_remote_copy(
            src_ref=src,
            dst_ref=dst,
            send_sem=face_send.at[step, s, p],
            recv_sem=face_recv.at[step, s, p],
            device_id=(around[s], me_c),
            device_id_type=MESH,
        )

    def row(step, t):
        return pltpu.make_async_remote_copy(
            src_ref=row_out.at[step, t],
            dst_ref=row_in.at[step, t],
            send_sem=row_send.at[step, t],
            recv_sem=row_recv.at[step, t],
            device_id=(me_l, side[t]),
            device_id_type=MESH,
        )

    def hop(s):
        return pltpu.make_async_remote_copy(
            src_ref=hop_out.at[s],
            dst_ref=relay.at[s],
            send_sem=hop_send.at[s],
            recv_sem=hop_recv.at[s],
            device_id=(around[s], me_c),
            device_id_type=MESH,
        )

    def forward(t):
        return pltpu.make_async_remote_copy(
            src_ref=relay,
            dst_ref=relay_in.at[t],
            send_sem=relay_send.at[t],
            recv_sem=relay_recv.at[t],
            device_id=(me_l, side[t]),
            device_id_type=MESH,
        )

    def edge(s, t):
        return pltpu.make_async_remote_copy(
            src_ref=edge_out.at[s, t],
            dst_ref=edge_in.at[s, t],
            send_sem=edge_send.at[s, t],
            recv_sem=edge_recv.at[s, t],
            device_id=(around[s], side[t]),
            device_id_type=MESH,
        )

    def pack_hop(s):
        for t in range(2):
            tile, r = ((0, 7), (nk + 1, 0))[t]
            for n, i in enumerate(EDGE_FIELDS[s][t]):
                m = 3 * t + n
                hop_out[s, m : m + 1] = f1[SLOT[i], (0, nx + 1)[s], tile, r : r + 1]

    def pass_edges():
        for s in range(2):
            hop(s).wait_recv()
        for t in range(2):

            @pl.when(has[t])
            def _():
                forward(t).start()

    def send_edge(s, t):
        tile, r = ((0, 0), (nk - 1, 7))[t]
        for n, i in enumerate(EDGE_FIELDS[s][t]):
            m = SLOT[i] - FACE[s][0]
            edge_out[s, t, n : n + 1] = stage[s, m, tile, r : r + 1]

        @pl.when(has[t])
        def _():
            edge(s, t).start()

    def get_edge(step, s, t):
        buf = (f1, f2)[step]
        if step == 1:

            @pl.when(has[1 - t])
            def _():
                edge(s, t).wait_recv()

        tile, r = ((nk, 7), (1, 0))[t]
        for n, i in enumerate(EDGE_FIELDS[s][t]):
            m = 3 * t + n
            value = relay_in[t, s, m : m + 1] if step == 0 else edge_in[s, t, n : n + 1]
            buf[SLOT[i], (nx, 1)[s], tile, r : r + 1] = value

    def pack_row(step, t):
        buf = (f1, f2)[step]
        tile, r = ((0, 7), (nk + 1, 0))[t]
        for n, i in enumerate(ROWS[t]):
            a = STATE[i][0]
            for x in range(max(a, 0), nx + min(a, 0)):
                row_out[step, t, n, x : x + 1] = buf[SLOT[i], x + 1, tile, r : r + 1]

    def send_row(step, t):
        @pl.when(has[t])
        def _():
            row(step, t).start()

    def get_row(step, t):
        buf = (f1, f2)[step]

        @pl.when(has[1 - t])
        def _():
            row(step, t).wait_recv()
            if step == 0:
                forward(t).wait_recv()

        tile, r = ((nk, 7), (1, 0))[t]
        for n, i in enumerate(ROWS[t]):
            a = STATE[i][0]
            for x in range(max(a, 0), nx + min(a, 0)):
                buf[SLOT[i], x + 1, tile, r : r + 1] = row_in[step, t, n, x : x + 1]

    def both(f, *args):
        for t in range(2):
            f(*args, t)

    def send_first(s):
        hop(s).start()
        face(0, s, 0).start()

    for s in (1, 0):
        wait_loads(faces[s])

        @pl.loop(0, nk, unroll=True)
        def _(k):
            first_step(faces[s], k)

        pack_hop(s)

        @pl.when(early)
        def _():
            if s == 1:
                wait_barrier()
            send_first(s)

    for t in range(2):

        @pl.loop(1, nx - 1, unroll=2)
        def _(x):
            if t == 0:
                wait_loads(x)
            first_step(x, ends[t])

        pack_row(0, t)
        pl.when(early)(lambda: send_row(0, t))

        @pl.when(late)
        def _():
            if t == 0:
                wait_barrier()
            send_row(0, t)
            if t == 0:
                for s in (1, 0):
                    send_first(s)

    @pl.loop(1, nx - 1)
    def _(x):
        @pl.loop(1, nk - 1)
        def _(k):
            first_step(x, k)

    @pl.when(ahead)
    def _():
        wait_barrier()
        for s in range(2):
            send_first(s)
        both(send_row, 0)
        for s in range(2):
            face(0, s, 1).start()

    pass_edges()

    @pl.when(level)
    def _():
        for s in (1, 0):
            face(0, s, 1).start()

    def outer(s, p):
        face(0, 1 - s, p).wait_recv()
        get_edge(0, 1 - s, 1 - p)

        @pl.loop(*pieces[p], unroll=True)
        def _(k):
            second_step(faces[s], k, s)

        send_edge(s, p)

    def between(p):
        @pl.loop(1, nx - 1)
        def _(x):
            second_step(x, ends[p])

        pack_row(1, p)
        send_row(1, p)

    for p in range(2):
        get_row(0, 1 - p)
        outer(1, p)
        face(1, 1, p).start()
        if p == 1:
            pl.when(behind)(lambda: face(1, 0, 0).start())
        outer(0, p)
        between(p)
        if p == 0:
            pl.when(jnp.logical_not(behind))(lambda: face(1, 0, 0).start())
        else:
            face(1, 0, 1).start()

    @pl.loop(1, nx - 1)
    def _(x):
        @pl.loop(1, nk - 1)
        def _(k):
            second_step(x, k)

    for p in range(2):
        for s in range(2):
            face(1, s, p).wait_recv()

            @pl.loop(*pieces[p])
            def _(k):
                for n in range(11):
                    put(f2, (nx - 1, 0)[s], k, ORDER[FACE[s][0] + n], arrived[s, n, k])

    for t in range(2):
        get_row(1, t)
        for s in range(2):
            get_edge(1, s, t)

    for s in range(2):
        hop(s).wait_send()
        for step in range(2):
            for p in range(2):
                face(step, s, p).wait_send()
    for t in range(2):

        @pl.when(has[t])
        def _():
            forward(t).wait_send()
            for s in range(2):
                row(s, t).wait_send()
                edge(s, t).wait_send()


GROUPS = [(0, 0, 9), (11, 9, 9), (30, 18, 9)]
SCAL_GROUPS = [(SLOT[27 + j], j, size) for j, size in ((0, 1), (1, 1), (2, 1), (3, 4), (7, 1), (8, 1), (9, 1), (10, 4))]


def store_kernel(nx, nk, f2, pop_hbm, scal_hbm, sem):
    copies = []
    for n, (slot, i, size) in enumerate(GROUPS):
        copies.append(
            pltpu.make_async_copy(
                f2.at[slot : slot + size, 1 : nx + 1, 1 : nk + 1],
                pop_hbm.at[i : i + size],
                sem.at[n],
            )
        )
    for n, (slot, j, size) in enumerate(SCAL_GROUPS):
        copies.append(
            pltpu.make_async_copy(
                f2.at[slot : slot + size, 1 : nx + 1, 1 : nk + 1],
                scal_hbm.at[j : j + size],
                sem.at[3 + n],
            )
        )
    for copy in copies:
        copy.start()
    for copy in copies:
        copy.wait()


def per_device(nl, nc, populations, scalars, node_flags):
    nx, ny, nz = node_flags.shape
    nk = ny // 8
    f32 = jnp.float32
    padded = (41, nx + 2, nk + 2, 8, nz)
    dma = pltpu.SemaphoreType.DMA
    place = pltpu.with_memory_space_constraint
    hbm = pl.BlockSpec(memory_space=pltpu.HBM)
    vmem = pl.BlockSpec(memory_space=pltpu.VMEM)
    f2 = pl.pallas_call(
        functools.partial(exchange_kernel, nl, nc, nx, nk),
        out_shape=pltpu.VMEM(padded, f32),
        in_specs=[hbm] * 3,
        out_specs=vmem,
        scratch_shapes=[
            pltpu.VMEM((27, nx, nk, 8, nz), f32),
            pltpu.VMEM((14, nx, nk, 8, nz), f32),
            pltpu.VMEM((nx, nk, 8, nz), jnp.int32),
            pltpu.VMEM(padded, f32),
            pltpu.VMEM((2, 11, nk, 8, nz), f32),
            pltpu.VMEM((2, 11, nk, 8, nz), f32),
            pltpu.VMEM((2, 2, 11, nx, nz), f32),
            pltpu.VMEM((2, 2, 11, nx, nz), f32),
            pltpu.VMEM((2, 8, nz), f32),
            pltpu.VMEM((2, 8, nz), f32),
            pltpu.VMEM((2, 2, 8, nz), f32),
            pltpu.VMEM((2, 2, 8, nz), f32),
            pltpu.VMEM((2, 2, 8, nz), f32),
            dma((3, nx)),
            dma((2, 2, 2)),
            dma((2, 2, 2)),
            dma((2, 2)),
            dma((2, 2)),
            dma((2,)),
            dma((2,)),
            dma((2,)),
            dma((2,)),
            dma((2, 2)),
            dma((2, 2)),
        ],
        compiler_params=pltpu.CompilerParams(
            collective_id=0, has_side_effects=True, vmem_limit_bytes=40 * 2**20
        ),
    )(
        place(populations.reshape(27, nx, nk, 8, nz), pltpu.HBM),
        place(scalars.reshape(14, nx, nk, 8, nz), pltpu.HBM),
        place(node_flags.reshape(nx, nk, 8, nz), pltpu.HBM),
    )
    new_pop, new_scal = pl.pallas_call(
        functools.partial(store_kernel, nx, nk),
        out_shape=(
            jax.ShapeDtypeStruct((27, nx, nk, 8, nz), f32),
            jax.ShapeDtypeStruct((14, nx, nk, 8, nz), f32),
        ),
        in_specs=[vmem],
        out_specs=(hbm, hbm),
        scratch_shapes=[dma((11,))],
        compiler_params=pltpu.CompilerParams(vmem_limit_bytes=2**20),
    )(place(f2, pltpu.VMEM))
    return new_pop.reshape(27, nx, ny, nz), new_scal.reshape(14, nx, ny, nz)


def solution(mesh):
    wide = P(None, "loop", "cross", None)
    return jax.shard_map(
        functools.partial(per_device, mesh.shape["loop"], mesh.shape["cross"]),
        mesh=mesh,
        in_specs=(wide, wide, P("loop", "cross", None)),
        out_specs=(wide, wide),
        check_vma=False,
    )
```
